256 devices in a mesh: src: 4 (over y), snk: 8 (over z_hi, x), slab: 8 (over z_lo, core).
Axes of the slice: x: 4, y: 4, z: 8 (z_hi: 2, z_lo: 4; z = z_hi * 4 + z_lo), core: 2. Of those that a mesh axis runs over, the one named last changes fastest.
Arguments:
- eigvecs: bfloat16 [16, 32768, 384], P('snk', ('src', 'slab')), may hold values from -0.09375 to 0.09375
- perambulator: bfloat16 [16, 8, 4, 192, 384], P('snk', 'src'), may hold values from -0.4375 to 0.4375
- momenta: int32 [4, 3], replicated, may hold values from 1 to 3
- source_times: int32 [8], P('src'), may hold values from 0 to 15, as said below
Outputs:
- blocks: float32 [4, 16, 8, 4, 192, 384], P(None, 'snk', 'src', None, 'slab')
The draws below stay inside these ranges and needn't reach their ends.
Inputs may be any that keep to these rules, and one draw needn't show every extreme that they name: `source_times`: distinct time slices.
All inputs are finite; a program needn't handle non-finite values.
Results may differ from the reference program's by a relative error of at most 0.0062.
Values may be sent and summed in bfloat16 or wider, within the bound.
A program may use at most 64 MiB of HBM per device.

```python
import math
import jax
import jax.numpy as jnp

LX = 32
LY = 32
NEV = 192
NMOM = 4
LZ = 32
NSITE = 32768
NT = 16
NSRC = 8


def draw_source_times(key, part):
    order = jax.random.permutation(jax.random.fold_in(key, 11), NT)
    return order[:NSRC].astype(jnp.int32)


def place_ends(result, own_key, least, top_value):
    index_at = [jax.random.randint(jax.random.fold_in(own_key, axis), (), 0, length) for axis, length in enumerate(result.shape)]
    main_axis = result.shape.index(max(result.shape))
    neighbour = index_at[:main_axis] + [(index_at[main_axis] + 1) % result.shape[main_axis]] + index_at[main_axis + 1:]
    return result.at[tuple(index_at)].set(least).at[tuple(neighbour)].set(top_value)


def levels(key, extent, shards, low, largest):
    factor_of, own = 1.0, jax.random.fold_in(key, 6)
    for dim, parts in shards:
        heights = jnp.exp(jax.random.uniform(jax.random.fold_in(own, dim), (parts,), jnp.float32, low / len(shards), largest / len(shards)))
        factor_of = factor_of * jnp.repeat(heights, extent[dim] // parts).reshape([-1 if axis == dim else 1 for axis in range(len(extent))])
    return factor_of


def scatter_about(own_key, dims, deviation, bound, shards=(), held_as=jnp.bfloat16):
    factor_of = levels(own_key, dims, shards, -0.22, 0.18) if shards else 1.0
    drawn = jax.random.normal(own_key, dims, jnp.float32) * deviation * factor_of
    return jnp.minimum(jnp.maximum(drawn, -bound), bound).astype(held_as)


def setup_inputs(seed: int = 0) -> dict:
    key_list = jax.random.split(jax.random.key(seed), 5)
    return {
        "eigvecs": scatter_about(key_list[0], (NT, NSITE, 2 * NEV), (0.22 / NSITE ** 0.25), 0.09375, ((0, 8), (1, 32))),
        "perambulator": scatter_about(key_list[1], (NT, NSRC, 4, NEV, 2 * NEV), NEV ** -0.5, 0.4375, ((0, 8), (1, 4))),
        "momenta": place_ends(jax.random.randint(key_list[2], (NMOM, 3), 1, 4), jax.random.fold_in(key_list[2], 1), 1, 3).astype(jnp.int32),
        "source_times": draw_source_times(jax.random.fold_in(key_list[4], 71), 0),
    }


def angles(momenta, xs, ys, zs, lz):
    fx = ((momenta[:, 0:1] * xs[None, :]) % LX).astype(jnp.float32) / LX
    fy = ((momenta[:, 1:2] * ys[None, :]) % LY).astype(jnp.float32) / LY
    fz = ((momenta[:, 2:3] * zs[None, :]) % lz).astype(jnp.float32) / lz
    return (2.0 * math.pi) * (fx + fy + fz)


def elemental(vec, angle):
    nev = vec.shape[1] // 2
    vf = vec.astype(jnp.float32)
    cosine = jnp.cos(angle)[:, None]
    sine = jnp.sin(angle)[:, None]
    vreal, vimag = vf[:, :nev], vf[:, nev:]
    phased = jnp.concatenate([cosine * vreal + sine * vimag, cosine * vimag - sine * vreal], axis=1).astype(jnp.bfloat16)
    gram = jnp.dot(vf.T, phased.astype(jnp.float32), preferred_element_type=jnp.float32)
    real = gram[:nev, :nev] + gram[nev:, nev:]
    imag = gram[:nev, nev:] - gram[nev:, :nev]
    return jnp.concatenate([real, imag], axis=1)


def reference(eigvecs, perambulator, momenta, source_times):
    nev = NEV
    sites = jnp.arange(NSITE, dtype=jnp.int32)
    xs = sites % LX
    ys = (sites // LX) % LY
    zs = sites // (LX * LY)
    angle = angles(momenta, xs, ys, zs, LZ)
    slices = []
    for t in range(NT):
        per_mom = [elemental(eigvecs[t], angle[m]) for m in range(NMOM)]
        slices.append(jnp.stack(per_mom, axis=0))
    phi = jnp.stack(slices, axis=0).astype(jnp.bfloat16)
    source = phi[source_times]
    tau = perambulator.astype(jnp.float32)
    outs = []
    for m in range(NMOM):
        sink = phi[:, m].astype(jnp.float32)
        stacked = jnp.concatenate([sink[:, :, :nev], sink[:, :, nev:]], axis=1)
        prod = jnp.einsum('tra,tsqab->tsqrb', stacked, tau)
        creal = prod[..., :nev, :nev] - prod[..., nev:, nev:]
        cimag = prod[..., :nev, nev:] + prod[..., nev:, :nev]
        half = jnp.concatenate([creal, cimag], axis=3).astype(jnp.bfloat16).astype(jnp.float32)
        src = source[:, m].astype(jnp.float32)
        both = jnp.concatenate([src[:, :, :nev], src[:, :, nev:]], axis=1)
        quad = jnp.einsum('tsqrb,scb->tsqrc', half, both)
        dreal = quad[..., :nev, :nev] + quad[..., nev:, nev:]
        dimag = quad[..., nev:, :nev] - quad[..., :nev, nev:]
        outs.append(jnp.concatenate([dreal, dimag], axis=-1))
    return jnp.stack(outs, axis=0)
```

```python
import math

import jax
import jax.numpy as jnp
from jax import lax
from jax.experimental import pallas as pl
from jax.experimental.pallas import tpu as pltpu
from jax.sharding import PartitionSpec as P

LX = 32
LY = 32
ZPL = 1
NX = 4
NY = 4
NZ = 8
ZLO = 4
MESH = pl.DeviceIdType.MESH
F32 = jnp.float32
BF16 = jnp.bfloat16


def angles(momenta, xs, ys, zs, lz):
    fx = (momenta[:, 0:1] * xs[None, :] % LX).astype(jnp.float32) / LX
    fy = (momenta[:, 1:2] * ys[None, :] % LY).astype(jnp.float32) / LY
    fz = (momenta[:, 2:3] * zs[None, :] % lz).astype(jnp.float32) / lz
    return 2.0 * math.pi * (fx + fy + fz)


def block_of(z):
    return lax.rem(z, ZLO) * 2 + lax.div(z, ZLO)


def exchange(part, st, sink, src, d2d, ysend, yrecv, q, zrecv, xall, stall, sel, srecv,
             d2d_s, d2d_r, st_s, st_r, y_s, y_r, z_s, z_r, x_s, x_r, sink_s, sink_r, sel_s, sel_r,
             ring_s, ring_r, sib_s, sib_r):
    y = lax.axis_index("src")
    snk = lax.axis_index("snk")
    slab = lax.axis_index("slab")
    zh, x = lax.div(snk, NX), lax.rem(snk, NX)
    zl, c = lax.div(slab, 2), lax.rem(slab, 2)
    z = zh * ZLO + zl
    own = block_of(z)

    def at(y=y, x=x, z=None, zh=zh, zl=zl, c=c):
        if z is not None:
            zh, zl = lax.div(z, ZLO), lax.rem(z, ZLO)
        return {"src": y, "snk": zh * NX + x, "slab": zl * 2 + c}

    def turn(value, by, size):
        return lax.rem(value + by, size)

    def copy(source, target, send, recv, device):
        return pltpu.make_async_remote_copy(
            src_ref=source, dst_ref=target, send_sem=send, recv_sem=recv, device_id=device, device_id_type=MESH
        )

    barrier = pltpu.get_barrier_semaphore()
    peers = [at(y=turn(y, k // 4, NY), zh=turn(zh, k // 2 % 2, 2), c=turn(c, k % 2, 2)) for k in range(1, 16)]
    peers += [at(z=turn(z, k, NZ)) for k in (1, 2, 3, 5, 6, 7)]
    peers += [at(x=turn(x, k, NX)) for k in (1, 2, 3)]
    for peer in peers:
        pl.semaphore_signal(barrier, inc=1, device_id=peer, device_id_type=MESH)
    pl.semaphore_wait(barrier, len(peers))

    sends = []
    sibling = at(c=1 - c)

    pair = {}
    for d in (1, 3, 2, 0):
        pair[d] = copy(part.at[1 - c, turn(y, d, NY)], d2d.at[d], d2d_s.at[d], d2d_r.at[d], sibling)
        pair[d].start()
        sends.append(pair[d])
    stall[y] = st[...]
    times = []
    for d in (1, 2, 3):
        times.append(copy(stall.at[y], stall.at[y], st_s.at[d - 1], st_r.at[turn(y, 0, NY)], at(y=turn(y, d, NY))))
        times[-1].start()
    sends += times

    along = []
    for d in (1, 3, 2):
        pair[d].wait_recv()
        ysend[d - 1] = (part[c, turn(y, d, NY)].astype(F32) + d2d[d].astype(F32)).astype(BF16)
        along.append(copy(ysend.at[d - 1], yrecv.at[d - 1], y_s.at[d - 1], y_r.at[d - 1], at(y=turn(y, d, NY))))
        along[-1].start()
    sends += along
    pair[0].wait_recv()
    for each in along:
        each.wait_recv()

    def summed(block):
        total = part[c, y, block].astype(F32) + d2d[0, block].astype(F32)
        for d in range(3):
            total += yrecv[d, block].astype(F32)
        return total.astype(BF16)

    for dz in (4, 3, 5, 2, 6, 1, 7):
        to = turn(z, dz, NZ)
        q[dz] = summed(block_of(to))
        each = copy(q.at[dz], zrecv.at[z], z_s.at[dz], z_r.at[z], at(z=to))
        each.start()
        sends.append(each)
    zrecv[z] = summed(own)
    for dz in range(1, NZ):
        come = turn(z, dz, NZ)
        copy(q.at[dz], zrecv.at[come], z_s.at[dz], z_r.at[come], at(z=come)).wait_recv()
    for g in range(2):
        total = zrecv[g * ZLO].astype(F32)
        for k in range(1, ZLO):
            total += zrecv[g * ZLO + k].astype(F32)
        xall[x, g] = total.astype(BF16)

    across = []
    for d in (1, 3, 2):
        across.append(copy(xall.at[x], xall.at[x], x_s.at[d - 1], x_r.at[x], at(x=turn(x, d, NX))))
        across[-1].start()
    sends += across

    for dy, dg in ((1, 0), (3, 0), (2, 0), (0, 1), (1, 1), (3, 1), (2, 1)):
        g = turn(zh, dg, 2)
        each = copy(xall.at[x, g], sink.at[c, y], sink_s.at[dy, dg], sink_r.at[c, y],
                    at(y=turn(y, dy, NY), zh=g, c=zh))
        each.start()
        sends.append(each)
    to_sibling = copy(xall.at[x, zh], sink.at[c, y], sink_s.at[0, 0], sink_r.at[c, y], sibling)

    @pl.when(c == zh)
    def _():
        sink[c, y] = xall[x, zh]

    @pl.when(c != zh)
    def _():
        to_sibling.start()

    for d in (1, 2, 3):
        come = turn(x, d, NX)
        copy(xall.at[come], xall.at[come], x_s.at[d - 1], x_r.at[come], at(x=come)).wait_recv()
    for d in (1, 2, 3):
        come = turn(y, d, NY)
        copy(stall.at[come], stall.at[come], st_s.at[d - 1], st_r.at[come], at(y=come)).wait_recv()

    def picked(plane, s):
        wanted = stall[plane, s][0:1]
        total = jnp.zeros((24, 384), F32)
        for k in range(NX):
            for g in range(2):
                total += jnp.where(wanted == 2 * (g * NX + k) + c, xall[k, g].astype(F32), 0.0)
        return total.astype(BF16)

    for dy, ds in ((1, 0), (1, 1), (3, 0), (3, 1), (2, 0), (2, 1), (0, 1)):
        plane, s = turn(y, dy, NY), turn(c, ds, 2)
        sel[dy, ds] = picked(plane, s)
        each = copy(sel.at[dy, ds], srecv.at[y, c], sel_s.at[dy, ds], sel_r.at[y, c], at(y=plane, c=s))
        each.start()
        sends.append(each)
    srecv[y, c] = picked(y, c)
    for dy, ds in ((1, 0), (1, 1), (3, 0), (3, 1), (2, 0), (2, 1), (0, 1)):
        m, k = turn(y, dy, NY), turn(c, ds, 2)
        copy(sel.at[dy, ds], srecv.at[m, k], sel_s.at[dy, ds], sel_r.at[m, k], at(y=m, c=k)).wait_recv()
    for m in range(NY):
        src[c, m, own] = srecv[m, 0] + srecv[m, 1]

    def rows(height, p):
        return src.at[c, pl.ds(2 * p, 2), block_of(height)]

    def hop(way, k, p):
        held = turn(z, NZ - (k - 1) if way == 0 else k - 1, NZ)
        to = turn(z, 1 if way == 0 else NZ - 1, NZ)
        return copy(rows(held, p), rows(held, p), ring_s.at[way, k - 1, p], ring_r.at[way, k - 1, p], at(z=to))

    def come(way, k, p):
        held = turn(z, NZ - k if way == 0 else k, NZ)
        to = turn(z, 1 if way == 0 else NZ - 1, NZ)
        copy(rows(held, p), rows(held, p), ring_s.at[way, k - 1, p], ring_r.at[way, k - 1, p], at(z=to)).wait_recv()

    siblings = []

    def share(slot, height, p):
        each = copy(rows(height, p), rows(height, p), sib_s.at[slot, p], sib_r.at[slot, p], sibling)
        each.start()
        sends.append(each)
        other = src.at[1 - c, pl.ds(2 * p, 2), block_of(height)]
        siblings.append(copy(other, other, sib_s.at[slot, p], sib_r.at[slot, p], sibling))

    def go(way, k, p):
        each = hop(way, k, p)
        each.start()
        sends.append(each)

    for p in range(2):
        go(0, 1, p)
        go(1, 1, p)
    for p in range(2):
        share(0, z, p)
    for k in (1, 2, 3):
        for p in range(2):
            for way in range(2):
                come(way, k, p)
                if k < 3 or p == way:
                    go(way, k + 1, p)
                share(k + 3 * way, turn(z, NZ - k if way == 0 else k, NZ), p)
    for way in range(2):
        come(way, 4, way)
        share(7, turn(z, 4, NZ), way)

    for each in siblings:
        each.wait_recv()
    for dy in range(NY):
        for dc in range(2):
            m, k = turn(y, dy, NY), turn(c, dc, 2)
            piece = copy(xall.at[x, 0], sink.at[k, m], sink_s.at[dy, dc], sink_r.at[k, m], at(y=m))
            if dy or dc:
                piece.wait_recv()
            else:
                pl.when(c != zh)(piece.wait_recv)
    for each in sends:
        each.wait_send()
    pl.when(c != zh)(to_sibling.wait_send)


def exchanged(part, st):
    dma = pltpu.SemaphoreType.DMA
    rows = (24, 384)

    def vmem(*lead):
        return pltpu.VMEM(lead + rows, BF16)

    whole = pl.BlockSpec(memory_space=pltpu.VMEM)
    return pl.pallas_call(
        exchange,
        out_shape=(jax.ShapeDtypeStruct((2, 4) + rows, BF16), jax.ShapeDtypeStruct((2, 4, 8) + rows, BF16)),
        in_specs=[whole, whole],
        out_specs=(whole, whole),
        scratch_shapes=[
            vmem(4, 8), vmem(3, 8), vmem(3, 8), vmem(8), vmem(8), vmem(4, 2), pltpu.VMEM((4, 2, 8, 384), jnp.int32),
            vmem(4, 2), vmem(4, 2),
            dma((4,)), dma((4,)), dma((3,)), dma((4,)), dma((3,)), dma((3,)), dma((8,)), dma((8,)),
            dma((3,)), dma((4,)), dma((4, 2)), dma((2, 4)), dma((4, 2)), dma((4, 2)),
            dma((2, 4, 2)), dma((2, 4, 2)), dma((8, 2)), dma((8, 2)),
        ],
        compiler_params=pltpu.CompilerParams(
            collective_id=0, has_side_effects=True, vmem_limit_bytes=48 * 1024 * 1024
        ),
    )(part, st)


def local(eigvecs, perambulator, momenta, source_times):
    nev = eigvecs.shape[2] // 2
    count = eigvecs.shape[1]
    slabs = lax.axis_size("slab")
    lz = ZPL * lax.axis_size("src") * slabs
    sites = jnp.arange(count, dtype=jnp.int32)
    xs = sites % LX
    ys = sites // LX % LY
    zs = sites // (LX * LY) + lax.axis_index(("src", "slab")) * ZPL
    angle = angles(momenta, xs, ys, zs, lz)
    vreal = eigvecs[:, :, :nev].astype(jnp.float32)
    vimag = eigvecs[:, :, nev:].astype(jnp.float32)
    partials = []
    for m in range(angle.shape[0]):
        cosine = jnp.cos(angle[m])[None, :, None]
        sine = jnp.sin(angle[m])[None, :, None]
        phased = jnp.concatenate(
            [cosine * vreal + sine * vimag, cosine * vimag - sine * vreal], axis=2
        ).astype(jnp.bfloat16)
        gram = jnp.einsum("tsa,tsb->tab", eigvecs, phased, preferred_element_type=jnp.float32)
        real = gram[:, :nev, :nev] + gram[:, nev:, nev:]
        imag = gram[:, :nev, nev:] - gram[:, nev:, :nev]
        partials.append(jnp.concatenate([real, imag], axis=2))
    part = jnp.stack(partials, axis=1).astype(jnp.bfloat16).reshape(2, 4, 8, 24, 384)
    st = jnp.broadcast_to(source_times[:, None, None], (2, 8, 384))
    sink, source = exchanged(part, st)
    rows = nev // slabs
    source = source.reshape(2, 4, nev, 2 * nev)
    stacked = jnp.concatenate([sink[..., :nev], sink[..., nev:]], axis=2)
    prod = jnp.einsum(
        "tmra,tsqab->mtsqrb", stacked, perambulator, preferred_element_type=jnp.float32
    )
    creal = prod[..., :rows, :nev] - prod[..., rows:, nev:]
    cimag = prod[..., :rows, nev:] + prod[..., rows:, :nev]
    half = jnp.concatenate([creal, cimag], axis=4).astype(jnp.bfloat16)
    both = jnp.concatenate([source[..., :nev], source[..., nev:]], axis=2)
    quad = jnp.einsum("mtsqrb,smcb->mtsqrc", half, both, preferred_element_type=jnp.float32)
    dreal = quad[..., :rows, :nev] + quad[..., rows:, nev:]
    dimag = quad[..., rows:, :nev] - quad[..., :rows, nev:]
    return jnp.concatenate([dreal, dimag], axis=-1)


def solution(mesh):
    placed = (P("snk", ("src", "slab"), None), P("snk", "src", None, None, None), P(), P("src"))
    return jax.shard_map(
        local,
        mesh=mesh,
        in_specs=placed,
        out_specs=P(None, "snk", "src", None, "slab", None),
        check_vma=False,
    )
```

```python
import math

import jax
import jax.numpy as jnp
from jax import lax
from jax.experimental import pallas as pl
from jax.experimental.pallas import tpu as pltpu
from jax.sharding import PartitionSpec as P

LX = 32
LY = 32
LZ = 32
NX = 4
NY = 4
NZ = 8
ZLO = 4
NEV = 192
COLS = 2 * NEV
SITES = LX * LY
ROWS = 24
MESH = pl.DeviceIdType.MESH
F32 = jnp.float32
BF16 = jnp.bfloat16


def block_of(z):
    return lax.rem(z, ZLO) * 2 + lax.div(z, ZLO)


def turned(columns):
    lane = lax.broadcasted_iota(jnp.int32, columns.shape, 1)
    return pltpu.roll(columns, NEV, 1) * jnp.where(lane < NEV, 1.0, -1.0)


def exchange(eig, mom, st, peram, src, half, trig, vt, vs, w, dsend, d2d, mine, ysend, yrecv, q, zrecv, eown, xall,
             stall, sel, srecv, sink, pcat,
             p_s, d2d_s, d2d_r, st_s, st_r, y_s, y_r, z_s, z_r, x_s, x_r, sink_s, sink_r, sel_s, sel_r,
             up_s, up_r, out_s, out_r, sib_s, sib_r):
    y = lax.axis_index("src")
    snk = lax.axis_index("snk")
    slab = lax.axis_index("slab")
    zh, x = lax.div(snk, NX), lax.rem(snk, NX)
    zl, c = lax.div(slab, 2), lax.rem(slab, 2)
    z = zh * ZLO + zl
    own = block_of(z)
    picks = x == y

    def at(y=y, x=x, z=None, zh=zh, zl=zl, c=c):
        if z is not None:
            zh, zl = lax.div(z, ZLO), lax.rem(z, ZLO)
        return {"src": y, "snk": zh * NX + x, "slab": zl * 2 + c}

    def turn(value, by, size):
        return lax.rem(value + by, size)

    def copy(source, target, send, recv, device):
        return pltpu.make_async_remote_copy(
            src_ref=source, dst_ref=target, send_sem=send, recv_sem=recv, device_id=device, device_id_type=MESH
        )

    barrier = pltpu.get_barrier_semaphore()
    peers = [at(y=turn(y, k // 4, NY), zh=turn(zh, k // 2 % 2, 2), c=turn(c, k % 2, 2)) for k in range(1, 16)]
    peers += [at(z=turn(z, k, NZ)) for k in (1, 2, 3, 5, 6, 7)]
    peers += [at(x=turn(x, k, NX)) for k in (1, 2, 3)]
    for peer in peers:
        pl.semaphore_signal(barrier, inc=1, device_id=peer, device_id_type=MESH)

    loads = []
    for t in range(2):
        for s in range(2):
            loads.append(pltpu.make_async_copy(peram.at[t, s], pcat.at[t, s, :, pl.ds(0, NEV)], p_s.at[t, s]))
            loads[-1].start()

    sends = []
    sibling = at(c=1 - c)

    row = lax.broadcasted_iota(jnp.int32, (8, SITES), 0)
    site = lax.broadcasted_iota(jnp.int32, (8, SITES), 1)

    def component(k):
        value = jnp.zeros((8, SITES), jnp.int32)
        for d in range(NY):
            value = jnp.where((row & 3) == d, mom[turn(y, d, NY), k], value)
        return value

    plane = y * NZ + slab
    fx = ((component(0) * (site & (LX - 1))) & (LX - 1)).astype(F32) / LX
    fy = ((component(1) * ((site >> 5) & (LY - 1))) & (LY - 1)).astype(F32) / LY
    fz = ((component(2) * plane) & (LZ - 1)).astype(F32) / LZ
    angle = 2.0 * math.pi * (fx + fy + fz)
    trig[...] = jnp.where(row < 4, jnp.cos(angle), jnp.sin(angle)).T

    def prepare(t):
        vt[t] = eig[t].T
        for r in range(0, SITES, 256):
            vs[t, r : r + 256] = turned(eig[t, r : r + 256].astype(F32)).astype(BF16)

    def elemental(t, d, slot):
        for r in range(0, SITES, 128):
            cosine = trig[r : r + 128, d : d + 1]
            sine = trig[r : r + 128, d + 4 : d + 5]
            phased = cosine * eig[t, r : r + 128].astype(F32) + sine * vs[t, r : r + 128].astype(F32)
            w[slot, r : r + 128] = phased.astype(BF16)
        gram = jnp.dot(vt[t], w[slot], preferred_element_type=F32)
        return (gram[:NEV] + turned(gram[NEV:])).reshape(NZ, ROWS, COLS)

    pair = {}

    def give(d):
        dsend[d] = elemental(1 - c, d, d % 2).astype(BF16)
        pair[d] = copy(dsend.at[d], d2d.at[d], d2d_s.at[d], d2d_r.at[d], sibling)

    prepare(1 - c)
    give(1)
    pl.semaphore_wait(barrier, len(peers))
    pair[1].start()
    stall[y] = st[...]
    to_pick = copy(stall.at[y], stall.at[y], st_s, st_r.at[y], at(y=x))
    pl.when(x != y)(to_pick.start)
    for d in (3, 2):
        give(d)
        pair[d].start()

    prepare(c)
    along = []
    for d in (1, 3, 2):
        value = elemental(c, d, d % 2)
        pair[d].wait_recv()
        ysend[d - 1] = (value + d2d[d].astype(F32)).astype(BF16)
        along.append(copy(ysend.at[d - 1], yrecv.at[d - 1], y_s.at[d - 1], y_r.at[d - 1], at(y=turn(y, d, NY))))
        along[-1].start()
    give(0)
    pair[0].start()
    sends += list(pair.values()) + along
    mine[...] = elemental(c, 0, 1)

    for each in loads:
        each.wait()
    at_row = lax.broadcasted_iota(jnp.int32, (COLS, COLS), 0)
    at_col = lax.broadcasted_iota(jnp.int32, (COLS, COLS), 1)
    swap = (jnp.where(at_col == at_row + NEV, 1.0, 0.0) - jnp.where(at_row == at_col + NEV, 1.0, 0.0)).astype(BF16)
    for t in range(2):
        for s in range(2):
            for k in range(4):
                pcat[t, s, k, NEV:] = jnp.dot(pcat[t, s, k, :NEV], swap, preferred_element_type=F32).astype(BF16)

    pair[0].wait_recv()
    for each in along:
        each.wait_recv()

    def summed(block):
        total = mine[block] + d2d[0, block].astype(F32)
        for d in range(3):
            total += yrecv[d, block].astype(F32)
        return total.astype(BF16)

    for dz in (4, 3, 5, 2, 6, 1, 7):
        to = turn(z, dz, NZ)
        q[dz] = summed(block_of(to))
        each = copy(q.at[dz], zrecv.at[z], z_s.at[dz], z_r.at[z], at(z=to))
        each.start()
        sends.append(each)
    zrecv[z] = summed(own)
    for dz in range(1, NZ):
        come = turn(z, dz, NZ)
        copy(q.at[dz], zrecv.at[come], z_s.at[dz], z_r.at[come], at(z=come)).wait_recv()
    for g in range(2):
        total = zrecv[g * ZLO].astype(F32)
        for k in range(1, ZLO):
            total += zrecv[g * ZLO + k].astype(F32)
        eown[g] = total.astype(BF16)

    to_diagonal = copy(eown, xall.at[x], x_s, x_r.at[x], at(x=y))
    pl.when(x != y)(to_diagonal.start)

    def picked(plane, s):
        wanted = stall[plane, s][0:1]
        total = jnp.zeros((ROWS, COLS), F32)
        for k in range(NX):
            for g in range(2):
                total += jnp.where(wanted == 2 * (g * NX + k) + c, xall[k, g].astype(F32), 0.0)
        return total.astype(BF16)

    def pick(dy, ds):
        return copy(sel.at[dy, ds], srecv.at[c], sel_s.at[dy, ds], sel_r.at[c], at(y=turn(y, dy, NY), c=turn(c, ds, 2)))

    moves = ((1, 0), (1, 1), (3, 0), (3, 1), (2, 0), (2, 1), (0, 1))

    @pl.when(picks)
    def _():
        xall[x] = eown[...]
        for d in (1, 2, 3):
            come = turn(x, d, NX)
            copy(eown, xall.at[come], x_s, x_r.at[come], at(x=come)).wait_recv()
            come = turn(y, d, NY)
            copy(stall.at[come], stall.at[come], st_s, st_r.at[come], at(y=come)).wait_recv()
        for dy, ds in moves:
            sel[dy, ds] = picked(turn(y, dy, NY), turn(c, ds, 2))
            pick(dy, ds).start()
        srecv[c] = picked(y, c)

    for dy, dg in ((1, 0), (3, 0), (2, 0), (0, 1), (1, 1), (3, 1), (2, 1)):
        g = turn(zh, dg, 2)
        each = copy(eown.at[g], sink.at[c, y], sink_s.at[dy, dg], sink_r.at[c, y], at(y=turn(y, dy, NY), zh=g, c=zh))
        each.start()
        sends.append(each)
    to_sibling = copy(eown.at[zh], sink.at[c, y], sink_s.at[0, 0], sink_r.at[c, y], sibling)

    @pl.when(c == zh)
    def _():
        sink[c, y] = eown[zh]

    @pl.when(c != zh)
    def _():
        to_sibling.start()

    def come_pick(k):
        copy(sel.at[0, 0], srecv.at[k], sel_s.at[0, 0], sel_r.at[k], at(y=x)).wait_recv()

    come_pick(1 - c)
    pl.when(x != y)(lambda: come_pick(c))
    src[c, x, own] = srecv[0] + srecv[1]

    groups = [(own, 1), (block_of(turn(z, ZLO, NZ)), 1)] + [(turn(zl, k, ZLO) * 2, 2) for k in (1, 2, 3)]

    def piece(s, m, group):
        first, count = groups[group]
        return src.at[s, m, pl.ds(first, count)]

    for dz in (4, 3, 5, 2, 6, 1, 7):
        each = copy(src.at[c, x, own], src.at[c, x, own], up_s.at[dz], up_r.at[z], at(z=turn(z, dz, NZ)))
        each.start()
        sends.append(each)

    def share(group, d):
        m = turn(x, NX - d, NX)
        each = copy(piece(c, m, group), piece(c, m, group), sib_s.at[d, group], sib_r.at[d, group], sibling)
        each.start()
        sends.append(each)

    def spread(group):
        for d in (1, 3, 2):
            each = copy(piece(c, x, group), piece(c, x, group), out_s.at[d - 1, group], out_r.at[d - 1, group],
                        at(x=turn(x, d, NX)))
            each.start()
            sends.append(each)
        share(group, 0)

    spread(0)

    for dy in range(NY):
        for dc in range(2):
            m, k = turn(y, dy, NY), turn(c, dc, 2)
            here = copy(eown.at[0], sink.at[k, m], sink_s.at[dy, dc], sink_r.at[k, m], at(y=m))
            if dy or dc:
                here.wait_recv()
            else:
                pl.when(c != zh)(here.wait_recv)
    for t in range(2):
        left = sink[t].astype(F32).reshape(NY * ROWS, COLS).astype(BF16)
        for s in range(2):
            for k in range(4):
                value = jnp.dot(left, pcat[t, s, k], preferred_element_type=F32)
                value = value.reshape(NY, ROWS, COLS).astype(BF16)
                for m in range(NY):
                    half[s, m, t, k] = value[m]

    def come_up(height):
        copy(src.at[c, x, own], src.at[c, x, block_of(height)], up_s.at[1], up_r.at[height], at(z=height)).wait_recv()

    come_up(turn(z, ZLO, NZ))
    spread(1)
    for k in (1, 3, 2):
        low = turn(zl, k, ZLO)
        come_up(low)
        come_up(low + ZLO)
        spread(1 + k)

    def come_out(group, d):
        m = turn(x, NX - d, NX)
        copy(piece(c, m, group), piece(c, m, group), out_s.at[d - 1, group], out_r.at[d - 1, group], at(x=m)).wait_recv()

    for group in (0, 1, 2, 4, 3):
        for d in (1, 3, 2):
            come_out(group, d)
            share(group, d)
    for group in range(5):
        for d in range(NX):
            m = turn(x, NX - d, NX)
            copy(piece(1 - c, m, group), piece(1 - c, m, group), sib_s.at[d, group], sib_r.at[d, group],
                 sibling).wait_recv()

    for each in sends:
        each.wait_send()
    pl.when(c != zh)(to_sibling.wait_send)

    @pl.when(x != y)
    def _():
        to_pick.wait_send()
        to_diagonal.wait_send()

    @pl.when(picks)
    def _():
        for dy, ds in moves:
            pick(dy, ds).wait_send()


def exchanged(eigvecs, momenta, st, perambulator):
    dma = pltpu.SemaphoreType.DMA

    def vmem(*lead, kind=BF16):
        return pltpu.VMEM(lead + (ROWS, COLS), kind)

    whole = pl.BlockSpec(memory_space=pltpu.VMEM)
    return pl.pallas_call(
        exchange,
        out_shape=(
            jax.ShapeDtypeStruct((2, NY, NZ, ROWS, COLS), BF16),
            jax.ShapeDtypeStruct((2, NY, 2, 4, ROWS, COLS), BF16),
        ),
        in_specs=[whole, pl.BlockSpec(memory_space=pltpu.SMEM), whole, pl.BlockSpec(memory_space=pl.ANY)],
        out_specs=(whole, whole),
        scratch_shapes=[
            pltpu.VMEM((SITES, 8), F32), pltpu.VMEM((2, COLS, SITES), BF16), pltpu.VMEM((2, SITES, COLS), BF16),
            pltpu.VMEM((2, SITES, COLS), BF16),
            vmem(4, 8), vmem(4, 8), vmem(8, kind=F32), vmem(3, 8), vmem(3, 8), vmem(8), vmem(8), vmem(2), vmem(4, 2),
            pltpu.VMEM((4, 2, 8, COLS), jnp.int32), vmem(4, 2), vmem(2), vmem(2, 4),
            pltpu.VMEM((2, 2, 4, COLS, COLS), BF16),
            dma((2, 2)), dma((4,)), dma((4,)), dma, dma((4,)), dma((3,)), dma((3,)), dma((8,)), dma((8,)),
            dma, dma((4,)), dma((4, 2)), dma((2, 4)), dma((4, 2)), dma((2,)),
            dma((8,)), dma((8,)), dma((3, 5)), dma((3, 5)), dma((4, 5)), dma((4, 5)),
        ],
        compiler_params=pltpu.CompilerParams(
            collective_id=0, has_side_effects=True, vmem_limit_bytes=48 * 1024 * 1024
        ),
    )(eigvecs, momenta, st, perambulator)


def product(half, src, out):
    at_row = lax.broadcasted_iota(jnp.int32, (COLS, COLS), 0)
    at_col = lax.broadcasted_iota(jnp.int32, (COLS, COLS), 1)
    swap = (jnp.where(at_col == at_row + NEV, 1.0, 0.0) - jnp.where(at_row == at_col + NEV, 1.0, 0.0)).astype(BF16)
    rows = src[0, 0]
    both = jnp.concatenate([rows, jnp.dot(rows, swap, preferred_element_type=F32).astype(BF16)], axis=0)
    value = lax.dot_general(half[0, 0], both, (((1,), (1,)), ((), ())), preferred_element_type=F32)
    out[0, :, 0] = value.reshape(2, 4, ROWS, COLS)


def local(eigvecs, perambulator, momenta, source_times):
    st = jnp.broadcast_to(source_times[:, None, None], (2, 8, COLS))
    source, half = exchanged(eigvecs, momenta, st, perambulator)
    block = pl.BlockSpec((1, 1, NEV, COLS), lambda m, s: (s, m, 0, 0))
    return pl.pallas_call(
        product,
        grid=(NY, 2),
        out_shape=jax.ShapeDtypeStruct((NY, 2, 2, 4, ROWS, COLS), F32),
        in_specs=[block, block],
        out_specs=pl.BlockSpec((1, 2, 1, 4, ROWS, COLS), lambda m, s: (m, 0, s, 0, 0, 0)),
    )(half.reshape(2, NY, NEV, COLS), source.reshape(2, NY, NEV, COLS))


def solution(mesh):
    placed = (P("snk", ("src", "slab"), None), P("snk", "src", None, None, None), P(), P("src"))
    return jax.shard_map(
        local,
        mesh=mesh,
        in_specs=placed,
        out_specs=P(None, "snk", "src", None, "slab", None),
        check_vma=False,
    )
```

```python
import math

import jax
import jax.numpy as jnp
from jax import lax
from jax.experimental import pallas as pl
from jax.experimental.pallas import tpu as pltpu
from jax.sharding import PartitionSpec as P

LX = 32
LY = 32
LZ = 32
NX = 4
NY = 4
NZ = 8
ZLO = 4
NEV = 192
COLS = 2 * NEV
SITES = LX * LY
ROWS = 24
MESH = pl.DeviceIdType.MESH
F32 = jnp.float32
BF16 = jnp.bfloat16


def block_of(z):
    return lax.rem(z, ZLO) * 2 + lax.div(z, ZLO)


def turned(columns):
    lane = lax.broadcasted_iota(jnp.int32, columns.shape, 1)
    return pltpu.roll(columns, NEV, 1) * jnp.where(lane < NEV, 1.0, -1.0)


def swap_matrix():
    at_row = lax.broadcasted_iota(jnp.int32, (COLS, COLS), 0)
    at_col = lax.broadcasted_iota(jnp.int32, (COLS, COLS), 1)
    return (jnp.where(at_col == at_row + NEV, 1.0, 0.0) - jnp.where(at_row == at_col + NEV, 1.0, 0.0)).astype(BF16)


def exchange(eigvecs, momenta, source_times, peram, blocks, src, half, both, made, eig, mom, st, trig, vt, vs, w, dsend, d2d, mine, ysend, yrecv, q, zrecv, eown, xall,
             stall, sel, srecv, sink, pcat,
             in_s, p_s, d2d_s, d2d_r, st_s, st_r, y_s, y_r, z_s, z_r, x_s, x_r, sink_s, sink_r, sel_s, sel_r,
             up_s, up_r, out_s, out_r, sib_s, sib_r, made_s):
    y = lax.axis_index("src")
    snk = lax.axis_index("snk")
    slab = lax.axis_index("slab")
    zh, x = lax.div(snk, NX), lax.rem(snk, NX)
    zl, c = lax.div(slab, 2), lax.rem(slab, 2)
    z = zh * ZLO + zl
    own = block_of(z)
    picks = x == y

    def at(y=y, x=x, z=None, zh=zh, zl=zl, c=c):
        if z is not None:
            zh, zl = lax.div(z, ZLO), lax.rem(z, ZLO)
        return {"src": y, "snk": zh * NX + x, "slab": zl * 2 + c}

    def turn(value, by, size):
        return lax.rem(value + by, size)

    def copy(source, target, send, recv, device):
        return pltpu.make_async_remote_copy(
            src_ref=source, dst_ref=target, send_sem=send, recv_sem=recv, device_id=device, device_id_type=MESH
        )

    barrier = pltpu.get_barrier_semaphore()
    peers = [at(y=turn(y, k // 4, NY), zh=turn(zh, k // 2 % 2, 2), c=turn(c, k % 2, 2)) for k in range(1, 16)]
    peers += [at(z=turn(z, k, NZ)) for k in (1, 2, 3, 5, 6, 7)]
    peers += [at(x=turn(x, k, NX)) for k in (1, 2, 3)]
    for peer in peers:
        pl.semaphore_signal(barrier, inc=1, device_id=peer, device_id_type=MESH)

    fetches = [
        pltpu.make_async_copy(momenta, mom, in_s.at[0]),
        pltpu.make_async_copy(source_times, st, in_s.at[1]),
        pltpu.make_async_copy(eigvecs.at[1 - c], eig.at[1 - c], in_s.at[2]),
        pltpu.make_async_copy(eigvecs.at[c], eig.at[c], in_s.at[3]),
    ]
    loads = []
    for t in range(2):
        for s in range(2):
            loads.append(pltpu.make_async_copy(peram.at[t, s], pcat.at[t, s, :, pl.ds(0, NEV)], p_s.at[t, s]))
    for each in fetches + loads:
        each.start()
    fetches[0].wait()

    sends = []
    sibling = at(c=1 - c)

    row = lax.broadcasted_iota(jnp.int32, (8, SITES), 0)
    site = lax.broadcasted_iota(jnp.int32, (8, SITES), 1)

    def component(k):
        value = jnp.zeros((8, SITES), jnp.int32)
        for d in range(NY):
            value = jnp.where((row & 3) == d, mom[turn(y, d, NY), k], value)
        return value

    plane = y * NZ + slab
    fx = ((component(0) * (site & (LX - 1))) & (LX - 1)).astype(F32) / LX
    fy = ((component(1) * ((site >> 5) & (LY - 1))) & (LY - 1)).astype(F32) / LY
    fz = ((component(2) * plane) & (LZ - 1)).astype(F32) / LZ
    angle = 2.0 * math.pi * (fx + fy + fz)
    trig[...] = jnp.where(row < 4, jnp.cos(angle), jnp.sin(angle)).T

    def prepare(t):
        vt[t] = eig[t].T
        for r in range(0, SITES, 256):
            vs[t, r : r + 256] = -jnp.dot(eig[t, r : r + 256], swap, preferred_element_type=F32).astype(BF16)

    def phase(t, d, slot):
        for r in range(0, SITES, 128):
            cosine = trig[r : r + 128, d : d + 1]
            sine = trig[r : r + 128, d + 4 : d + 5]
            phased = cosine * eig[t, r : r + 128].astype(F32) + sine * vs[t, r : r + 128].astype(F32)
            w[slot, r : r + 128] = phased.astype(BF16)

    swap = swap_matrix()
    fetches[2].wait()
    prepare(1 - c)
    fetches[3].wait()
    prepare(c)

    pair = {}
    along = {}
    turns = ((1, 2), (1, 1), (0, 2), (1, 3), (0, 1), (0, 3), (1, 0), (0, 0))

    def time(other):
        return 1 - c if other else c

    def go_along(d):
        pair[d].wait_recv()
        ysend[d - 1] = (mine[d] + d2d[d].astype(F32)).astype(BF16)
        along[d] = copy(ysend.at[d - 1], yrecv.at[d - 1], y_s.at[d - 1], y_r.at[d - 1], at(y=turn(y, d, NY)))
        along[d].start()

    phase(1 - c, 2, 0)
    for k, (other, d) in enumerate(turns):
        if k + 1 < len(turns):
            phase(time(turns[k + 1][0]), turns[k + 1][1], (k + 1) % 2)
        gram = jnp.dot(vt[time(other)], w[k % 2], preferred_element_type=F32)
        value = (gram[:NEV] + turned(gram[NEV:])).reshape(NZ, ROWS, COLS)
        if other:
            dsend[d] = value.astype(BF16)
            pair[d] = copy(dsend.at[d], d2d.at[d], d2d_s.at[d], d2d_r.at[d], sibling)
        else:
            mine[d] = value
        if k == 3:
            pl.semaphore_wait(barrier, len(peers))
            for each in (2, 1, 3):
                pair[each].start()
            fetches[1].wait()
            for s in range(2):
                stall[y, s] = jnp.full((8, COLS), st[s], jnp.int32)
            to_pick = copy(stall.at[y], stall.at[y], st_s, st_r.at[y], at(y=x))
            pl.when(x != y)(to_pick.start)
        if k == 4:
            go_along(2)
            go_along(1)
        if k == 5:
            go_along(3)
        if k == 6:
            pair[0].start()
    along = [along[d] for d in (2, 1, 3)]
    sends += list(pair.values()) + along

    for each in loads:
        each.wait()
    for t in range(2):
        for s in range(2):
            for k in range(4):
                pcat[t, s, k, NEV:] = jnp.dot(pcat[t, s, k, :NEV], swap, preferred_element_type=F32).astype(BF16)

    pair[0].wait_recv()
    for each in along:
        each.wait_recv()

    def summed(block):
        total = mine[0, block] + d2d[0, block].astype(F32)
        for d in range(3):
            total += yrecv[d, block].astype(F32)
        return total.astype(BF16)

    for dz in (4, 3, 5, 2, 6, 1, 7):
        to = turn(z, dz, NZ)
        q[dz] = summed(block_of(to))
        each = copy(q.at[dz], zrecv.at[z], z_s.at[dz], z_r.at[z], at(z=to))
        each.start()
        sends.append(each)
    zrecv[z] = summed(own)
    for dz in range(1, NZ):
        come = turn(z, dz, NZ)
        copy(q.at[dz], zrecv.at[come], z_s.at[dz], z_r.at[come], at(z=come)).wait_recv()
    for g in range(2):
        total = zrecv[g * ZLO].astype(F32)
        for k in range(1, ZLO):
            total += zrecv[g * ZLO + k].astype(F32)
        eown[g] = total.astype(BF16)

    to_diagonal = copy(eown, xall.at[x], x_s, x_r.at[x], at(x=y))
    pl.when(x != y)(to_diagonal.start)

    for dy, dg in ((1, 0), (3, 0), (2, 0), (0, 1), (1, 1), (3, 1), (2, 1)):
        g = turn(zh, dg, 2)
        each = copy(eown.at[g], sink.at[c, y], sink_s.at[dy, dg], sink_r.at[c, y], at(y=turn(y, dy, NY), zh=g, c=zh))
        each.start()
        sends.append(each)
    to_sibling = copy(eown.at[zh], sink.at[c, y], sink_s.at[0, 0], sink_r.at[c, y], sibling)

    @pl.when(c == zh)
    def _():
        sink[c, y] = eown[zh]

    @pl.when(c != zh)
    def _():
        to_sibling.start()

    def picked(plane, s):
        wanted = stall[plane, s][0:1]
        total = jnp.zeros((ROWS, COLS), F32)
        for k in range(NX):
            for g in range(2):
                total += jnp.where(wanted == 2 * (g * NX + k) + c, xall[k, g].astype(F32), 0.0)
        return total.astype(BF16)

    def pick(dy, ds):
        return copy(sel.at[dy, ds], srecv.at[c], sel_s.at[dy, ds], sel_r.at[c], at(y=turn(y, dy, NY), c=turn(c, ds, 2)))

    moves = ((1, 0), (1, 1), (3, 0), (3, 1), (2, 0), (2, 1), (0, 1))

    @pl.when(picks)
    def _():
        xall[x] = eown[...]
        for d in (1, 2, 3):
            come = turn(x, d, NX)
            copy(eown, xall.at[come], x_s, x_r.at[come], at(x=come)).wait_recv()
            come = turn(y, d, NY)
            copy(stall.at[come], stall.at[come], st_s, st_r.at[come], at(y=come)).wait_recv()
        for dy, ds in moves:
            sel[dy, ds] = picked(turn(y, dy, NY), turn(c, ds, 2))
            pick(dy, ds).start()
        srecv[c] = picked(y, c)

    def come_pick(k):
        copy(sel.at[0, 0], srecv.at[k], sel_s.at[0, 0], sel_r.at[k], at(y=x)).wait_recv()

    come_pick(1 - c)
    pl.when(x != y)(lambda: come_pick(c))
    src[c, x, own] = srecv[0] + srecv[1]

    order = (0, 1, 7, 2, 6, 3, 5, 4)

    def piece(s, m, group):
        return src.at[s, m, block_of(turn(z, order[group], NZ))]

    for dz in (4, 3, 5, 2, 6, 1, 7):
        each = copy(src.at[c, x, own], src.at[c, x, own], up_s.at[dz], up_r.at[z], at(z=turn(z, dz, NZ)))
        each.start()
        sends.append(each)

    def share(group, d):
        m = turn(x, NX - d, NX)
        each = copy(piece(c, m, group), piece(c, m, group), sib_s.at[d, group], sib_r.at[d, group], sibling)
        each.start()
        sends.append(each)

    def spread(group):
        for d in (1, 3, 2):
            each = copy(piece(c, x, group), piece(c, x, group), out_s.at[d - 1, group], out_r.at[d - 1, group],
                        at(x=turn(x, d, NX)))
            each.start()
            sends.append(each)
        share(group, 0)

    spread(0)

    for dy in range(NY):
        for dc in range(2):
            m, k = turn(y, dy, NY), turn(c, dc, 2)
            here = copy(eown.at[0], sink.at[k, m], sink_s.at[dy, dc], sink_r.at[k, m], at(y=m))
            if dy or dc:
                here.wait_recv()
            else:
                pl.when(c != zh)(here.wait_recv)
    for t in range(2):
        left = sink[t].astype(F32).reshape(NY * ROWS, COLS).astype(BF16)
        for s in range(2):
            for k in range(4):
                value = jnp.dot(left, pcat[t, s, k], preferred_element_type=F32)
                value = value.reshape(NY, ROWS, COLS).astype(BF16)
                for m in range(NY):
                    half[s, m, 4 * t + k] = value[m]

    def come_up(height):
        copy(src.at[c, x, own], src.at[c, x, block_of(height)], up_s.at[1], up_r.at[height], at(z=height)).wait_recv()

    for group in range(1, NZ):
        come_up(turn(z, order[group], NZ))
        spread(group)

    def come_out(group, d):
        m = turn(x, NX - d, NX)
        copy(piece(c, m, group), piece(c, m, group), out_s.at[d - 1, group], out_r.at[d - 1, group], at(x=m)).wait_recv()

    def come_shared(group, d):
        m = turn(x, NX - d, NX)
        copy(piece(1 - c, m, group), piece(1 - c, m, group), sib_s.at[d, group], sib_r.at[d, group], sibling).wait_recv()

    written = []

    def flat(value):
        return value.astype(F32).reshape(NEV, COLS).astype(BF16)

    def finish(s, d):
        slot, m = len(written), turn(x, NX - d, NX)
        rows = flat(src[s, m])
        both[slot % 2, :NEV] = rows
        both[slot % 2, NEV:] = jnp.dot(rows, swap, preferred_element_type=F32).astype(BF16)
        value = lax.dot_general(
            flat(half[s, m]), both[slot % 2], (((1,), (1,)), ((), ())), preferred_element_type=F32
        )
        made[slot] = value.reshape(2, 4, ROWS, COLS)
        written.append(pltpu.make_async_copy(made.at[slot], blocks.at[m, :, s], made_s.at[slot]))
        written[-1].start()

    early = 3
    for group in range(early):
        for d in (1, 3, 2):
            come_out(group, d)
            share(group, d)
    finish(c, 0)
    for group in range(NZ):
        come_shared(group, 0)
    finish(1 - c, 0)
    for group in range(early, NZ):
        for d in (1, 3, 2):
            come_out(group, d)
            share(group, d)
    for d in (1, 3, 2):
        finish(c, d)
    for d in (1, 3, 2):
        for group in range(NZ):
            come_shared(group, d)
        finish(1 - c, d)

    for each in written:
        each.wait()
    for each in sends:
        each.wait_send()
    pl.when(c != zh)(to_sibling.wait_send)

    @pl.when(x != y)
    def _():
        to_pick.wait_send()
        to_diagonal.wait_send()

    @pl.when(picks)
    def _():
        for dy, ds in moves:
            pick(dy, ds).wait_send()


def exchanged(eigvecs, momenta, source_times, perambulator):
    dma = pltpu.SemaphoreType.DMA

    def vmem(*lead, kind=BF16):
        return pltpu.VMEM(lead + (ROWS, COLS), kind)

    return pl.pallas_call(
        exchange,
        out_shape=jax.ShapeDtypeStruct((NY, 2, 2, 4, ROWS, COLS), F32),
        in_specs=[pl.BlockSpec(memory_space=pltpu.HBM)] * 4,
        out_specs=pl.BlockSpec(memory_space=pltpu.HBM),
        scratch_shapes=[
            vmem(2, 4, 8), vmem(2, 4, 8), pltpu.VMEM((2, COLS, COLS), BF16), vmem(8, 2, 4, kind=F32),
            pltpu.VMEM((2, SITES, COLS), BF16), pltpu.SMEM((NY, 3), jnp.int32), pltpu.SMEM((2,), jnp.int32),
            pltpu.VMEM((SITES, 8), F32), pltpu.VMEM((2, COLS, SITES), BF16), pltpu.VMEM((2, SITES, COLS), BF16),
            pltpu.VMEM((2, SITES, COLS), BF16),
            vmem(4, 8), vmem(4, 8), vmem(4, 8, kind=F32), vmem(3, 8), vmem(3, 8), vmem(8), vmem(8), vmem(2), vmem(4, 2),
            pltpu.VMEM((4, 2, 8, COLS), jnp.int32), vmem(4, 2), vmem(2), vmem(2, 4),
            pltpu.VMEM((2, 2, 4, COLS, COLS), BF16),
            dma((4,)), dma((2, 2)), dma((4,)), dma((4,)), dma, dma((4,)), dma((3,)), dma((3,)), dma((8,)), dma((8,)),
            dma, dma((4,)), dma((4, 2)), dma((2, 4)), dma((4, 2)), dma((2,)),
            dma((8,)), dma((8,)), dma((3, 8)), dma((3, 8)), dma((4, 8)), dma((4, 8)), dma((8,)),
        ],
        compiler_params=pltpu.CompilerParams(
            collective_id=0, has_side_effects=True, vmem_limit_bytes=58 * 1024 * 1024
        ),
    )(eigvecs, momenta, source_times, perambulator)


def local(eigvecs, perambulator, momenta, source_times):
    return exchanged(eigvecs, momenta, source_times, perambulator)


def solution(mesh):
    placed = (P("snk", ("src", "slab"), None), P("snk", "src", None, None, None), P(), P("src"))
    return jax.shard_map(
        local,
        mesh=mesh,
        in_specs=placed,
        out_specs=P(None, "snk", "src", None, "slab", None),
        check_vma=False,
    )
```

```python
import math

import jax
import jax.numpy as jnp
from jax import lax
from jax.experimental import pallas as pl
from jax.experimental.pallas import tpu as pltpu
from jax.sharding import PartitionSpec as P

LX = 32
LY = 32
LZ = 32
NX = 4
NY = 4
NZ = 8
ZLO = 4
NEV = 192
COLS = 2 * NEV
SITES = LX * LY
ROWS = 24
MESH = pl.DeviceIdType.MESH
F32 = jnp.float32
BF16 = jnp.bfloat16


def block_of(z):
    return lax.rem(z, ZLO) * 2 + lax.div(z, ZLO)


def turned(columns):
    lane = lax.broadcasted_iota(jnp.int32, columns.shape, 1)
    return pltpu.roll(columns, NEV, 1) * jnp.where(lane < NEV, 1.0, -1.0)


def swap_matrix():
    at_row = lax.broadcasted_iota(jnp.int32, (COLS, COLS), 0)
    at_col = lax.broadcasted_iota(jnp.int32, (COLS, COLS), 1)
    return (jnp.where(at_col == at_row + NEV, 1.0, 0.0) - jnp.where(at_row == at_col + NEV, 1.0, 0.0)).astype(BF16)


def exchange(eigvecs, momenta, source_times, peram, blocks, src, half, both, eig, mom, st, trig, vt, vs, w, dsend, d2d, mine, ysend, yrecv, q, zrecv, eown, xall,
             stall, sel, srecv, sink, pcat,
             in_s, p_s, d2d_s, d2d_r, st_s, st_r, y_s, y_r, z_s, z_r, x_s, x_r, sink_s, sink_r, sel_s, sel_r,
             up_s, up_r, out_s, out_r, sib_s, sib_r):
    y = lax.axis_index("src")
    snk = lax.axis_index("snk")
    slab = lax.axis_index("slab")
    zh, x = lax.div(snk, NX), lax.rem(snk, NX)
    zl, c = lax.div(slab, 2), lax.rem(slab, 2)
    z = zh * ZLO + zl
    own = block_of(z)
    picks = x == y

    def at(y=y, x=x, z=None, zh=zh, zl=zl, c=c):
        if z is not None:
            zh, zl = lax.div(z, ZLO), lax.rem(z, ZLO)
        return {"src": y, "snk": zh * NX + x, "slab": zl * 2 + c}

    def turn(value, by, size):
        return lax.rem(value + by, size)

    def copy(source, target, send, recv, device):
        return pltpu.make_async_remote_copy(
            src_ref=source, dst_ref=target, send_sem=send, recv_sem=recv, device_id=device, device_id_type=MESH
        )

    barrier = pltpu.get_barrier_semaphore()
    peers = [at(y=turn(y, k // 4, NY), zh=turn(zh, k // 2 % 2, 2), c=turn(c, k % 2, 2)) for k in range(1, 16)]
    peers += [at(z=turn(z, k, NZ)) for k in (1, 2, 3, 5, 6, 7)]
    peers += [at(x=turn(x, k, NX)) for k in (1, 2, 3)]
    for peer in peers:
        pl.semaphore_signal(barrier, inc=1, device_id=peer, device_id_type=MESH)

    fetches = [
        pltpu.make_async_copy(momenta, mom, in_s.at[0]),
        pltpu.make_async_copy(source_times, st, in_s.at[1]),
        pltpu.make_async_copy(eigvecs.at[1 - c], eig.at[1 - c], in_s.at[2]),
        pltpu.make_async_copy(eigvecs.at[c], eig.at[c], in_s.at[3]),
    ]
    loads = []
    for t in range(2):
        for s in range(2):
            loads.append(pltpu.make_async_copy(peram.at[t, s], pcat.at[t, s, :, pl.ds(0, NEV)], p_s.at[t, s]))
    for each in fetches:
        each.start()
    fetches[0].wait()

    sends = []
    sibling = at(c=1 - c)

    row = lax.broadcasted_iota(jnp.int32, (8, SITES), 0)
    site = lax.broadcasted_iota(jnp.int32, (8, SITES), 1)

    def component(k):
        value = jnp.zeros((8, SITES), jnp.int32)
        for d in range(NY):
            value = jnp.where((row & 3) == d, mom[turn(y, d, NY), k], value)
        return value

    plane = y * NZ + slab
    fx = ((component(0) * (site & (LX - 1))) & (LX - 1)).astype(F32) / LX
    fy = ((component(1) * ((site >> 5) & (LY - 1))) & (LY - 1)).astype(F32) / LY
    fz = ((component(2) * plane) & (LZ - 1)).astype(F32) / LZ
    angle = 2.0 * math.pi * (fx + fy + fz - jnp.where(row < 4, 0.0, 0.25))
    trig[...] = jnp.cos(angle).T

    def prepare(t):
        vt[t] = eig[t].T
        for r in range(0, SITES, 256):
            vs[t, r : r + 256] = -jnp.dot(eig[t, r : r + 256], swap, preferred_element_type=F32).astype(BF16)

    def phase(t, d, slot):
        for r in range(0, SITES, 128):
            cosine = trig[r : r + 128, d : d + 1]
            sine = trig[r : r + 128, d + 4 : d + 5]
            phased = cosine * eig[t, r : r + 128].astype(F32) + sine * vs[t, r : r + 128].astype(F32)
            w[slot, r : r + 128] = phased.astype(BF16)

    swap = swap_matrix()
    fetches[2].wait()
    prepare(1 - c)

    pair = {}
    along = {}
    turns = ((1, 2), (1, 1), (0, 2), (1, 3), (0, 1), (0, 3), (1, 0), (0, 0))

    def time(other):
        return 1 - c if other else c

    def go_along(d):
        pair[d].wait_recv()
        ysend[d - 1] = (mine[d] + d2d[d].astype(F32)).astype(BF16)
        along[d] = copy(ysend.at[d - 1], yrecv.at[d - 1], y_s.at[d - 1], y_r.at[d - 1], at(y=turn(y, d, NY)))
        along[d].start()

    phase(1 - c, 2, 0)
    for k, (other, d) in enumerate(turns):
        if k == 1:
            fetches[3].wait()
            for each in loads:
                each.start()
            prepare(c)
        if k + 1 < len(turns):
            phase(time(turns[k + 1][0]), turns[k + 1][1], (k + 1) % 2)
        gram = jnp.dot(vt[time(other)], w[k % 2], preferred_element_type=F32)
        value = (gram[:NEV] + turned(gram[NEV:])).reshape(NZ, ROWS, COLS)
        if other:
            dsend[d] = value.astype(BF16)
            pair[d] = copy(dsend.at[d], d2d.at[d], d2d_s.at[d], d2d_r.at[d], sibling)
        else:
            mine[d] = value
        if k == 1:
            pl.semaphore_wait(barrier, len(peers))
            for each in (2, 1):
                pair[each].start()
            fetches[1].wait()
            for s in range(2):
                stall[y, s] = jnp.full((8, COLS), st[s], jnp.int32)
            to_pick = copy(stall.at[y], stall.at[y], st_s, st_r.at[y], at(y=x))
            pl.when(x != y)(to_pick.start)
        elif k and other:
            pair[d].start()
        elif k and d:
            go_along(d)
    along = [along[d] for d in (2, 1, 3)]
    sends += list(pair.values()) + along

    for each in loads:
        each.wait()
    for t in range(2):
        for s in range(2):
            for k in range(4):
                pcat[t, s, k, NEV:] = jnp.dot(pcat[t, s, k, :NEV], swap, preferred_element_type=F32).astype(BF16)

    pair[0].wait_recv()
    for each in along:
        each.wait_recv()

    def summed(block):
        total = mine[0, block] + d2d[0, block].astype(F32)
        for d in range(3):
            total += yrecv[d, block].astype(F32)
        return total.astype(BF16)

    for dz in (4, 3, 5, 2, 6, 1, 7):
        to = turn(z, dz, NZ)
        q[dz] = summed(block_of(to))
        each = copy(q.at[dz], zrecv.at[z], z_s.at[dz], z_r.at[z], at(z=to))
        each.start()
        sends.append(each)
    zrecv[z] = summed(own)
    for dz in range(1, NZ):
        come = turn(z, dz, NZ)
        copy(q.at[dz], zrecv.at[come], z_s.at[dz], z_r.at[come], at(z=come)).wait_recv()
    for g in range(2):
        total = zrecv[g * ZLO].astype(F32)
        for k in range(1, ZLO):
            total += zrecv[g * ZLO + k].astype(F32)
        eown[g] = total.astype(BF16)

    to_diagonal = copy(eown, xall.at[x], x_s, x_r.at[x], at(x=y))
    pl.when(x != y)(to_diagonal.start)

    for dy, dg in ((1, 0), (3, 0), (2, 0), (0, 1), (1, 1), (3, 1), (2, 1)):
        g = turn(zh, dg, 2)
        each = copy(eown.at[g], sink.at[c, y], sink_s.at[dy, dg], sink_r.at[c, y], at(y=turn(y, dy, NY), zh=g, c=zh))
        each.start()
        sends.append(each)
    to_sibling = copy(eown.at[zh], sink.at[c, y], sink_s.at[0, 0], sink_r.at[c, y], sibling)

    @pl.when(c == zh)
    def _():
        sink[c, y] = eown[zh]

    @pl.when(c != zh)
    def _():
        to_sibling.start()

    def picked(plane, s):
        wanted = stall[plane, s][0:1]
        total = jnp.zeros((ROWS, COLS), F32)
        for k in range(NX):
            for g in range(2):
                total += jnp.where(wanted == 2 * (g * NX + k) + c, xall[k, g].astype(F32), 0.0)
        return total.astype(BF16)

    def pick(dy, ds):
        return copy(sel.at[dy, ds], srecv.at[c], sel_s.at[dy, ds], sel_r.at[c], at(y=turn(y, dy, NY), c=turn(c, ds, 2)))

    moves = ((1, 0), (1, 1), (3, 0), (3, 1), (2, 0), (2, 1), (0, 1))

    @pl.when(picks)
    def _():
        xall[x] = eown[...]
        for d in (1, 2, 3):
            come = turn(x, d, NX)
            copy(eown, xall.at[come], x_s, x_r.at[come], at(x=come)).wait_recv()
            come = turn(y, d, NY)
            copy(stall.at[come], stall.at[come], st_s, st_r.at[come], at(y=come)).wait_recv()
        for dy, ds in moves:
            sel[dy, ds] = picked(turn(y, dy, NY), turn(c, ds, 2))
            pick(dy, ds).start()
        srecv[c] = picked(y, c)

    def come_pick(k):
        copy(sel.at[0, 0], srecv.at[k], sel_s.at[0, 0], sel_r.at[k], at(y=x)).wait_recv()

    come_pick(1 - c)
    pl.when(x != y)(lambda: come_pick(c))
    src[c, x, own] = srecv[0] + srecv[1]

    order = (0, 1, 7, 2, 6, 3, 5, 4)

    def piece(s, m, group):
        return src.at[s, m, block_of(turn(z, order[group], NZ))]

    for dz in (4, 3, 5, 2, 6, 1, 7):
        each = copy(src.at[c, x, own], src.at[c, x, own], up_s.at[dz], up_r.at[z], at(z=turn(z, dz, NZ)))
        each.start()
        sends.append(each)

    def share(group, d):
        m = turn(x, NX - d, NX)
        each = copy(piece(c, m, group), piece(c, m, group), sib_s.at[d, group], sib_r.at[d, group], sibling)
        each.start()
        sends.append(each)

    def spread(group):
        for d in (1, 3, 2):
            each = copy(piece(c, x, group), piece(c, x, group), out_s.at[d - 1, group], out_r.at[d - 1, group],
                        at(x=turn(x, d, NX)))
            each.start()
            sends.append(each)
        share(group, 0)

    spread(0)

    def come_up(height):
        copy(src.at[c, x, own], src.at[c, x, block_of(height)], up_s.at[1], up_r.at[height], at(z=height)).wait_recv()

    for group in range(1, NZ):
        come_up(turn(z, order[group], NZ))
        spread(group)

    for dy in range(NY):
        for dc in range(2):
            m, k = turn(y, dy, NY), turn(c, dc, 2)
            here = copy(eown.at[0], sink.at[k, m], sink_s.at[dy, dc], sink_r.at[k, m], at(y=m))
            if dy or dc:
                here.wait_recv()
            else:
                pl.when(c != zh)(here.wait_recv)
    for t in range(2):
        left = sink[t].astype(F32).reshape(NY * ROWS, COLS).astype(BF16)
        for s in range(2):
            for k in range(4):
                value = jnp.dot(left, pcat[t, s, k], preferred_element_type=F32)
                value = value.reshape(NY, ROWS, COLS).astype(BF16)
                for m in range(NY):
                    half[s, m, 4 * t + k] = value[m]

    def come_out(group, d):
        m = turn(x, NX - d, NX)
        copy(piece(c, m, group), piece(c, m, group), out_s.at[d - 1, group], out_r.at[d - 1, group], at(x=m)).wait_recv()

    def come_shared(group, d):
        m = turn(x, NX - d, NX)
        copy(piece(1 - c, m, group), piece(1 - c, m, group), sib_s.at[d, group], sib_r.at[d, group], sibling).wait_recv()


    def flat(value):
        return value.astype(F32).reshape(NEV, COLS).astype(BF16)

    def finish(s, d):
        slot, m = d, turn(x, NX - d, NX)
        rows = flat(src[s, m])
        both[slot % 2, :NEV] = rows
        both[slot % 2, NEV:] = jnp.dot(rows, swap, preferred_element_type=F32).astype(BF16)
        value = lax.dot_general(
            flat(half[s, m]), both[slot % 2], (((1,), (1,)), ((), ())), preferred_element_type=F32
        )
        value = value.reshape(2, 4, ROWS, COLS)
        for t in range(2):
            blocks[m, t, s] = value[t]

    early = 3
    for group in range(early):
        for d in (1, 3, 2):
            come_out(group, d)
            share(group, d)
    finish(c, 0)
    for group in range(NZ):
        come_shared(group, 0)
    finish(1 - c, 0)
    for group in range(early, NZ):
        for d in (1, 3, 2):
            come_out(group, d)
            share(group, d)
    for d in (1, 3, 2):
        finish(c, d)
    for d in (1, 3, 2):
        for group in range(NZ):
            come_shared(group, d)
        finish(1 - c, d)

    for each in sends:
        each.wait_send()
    pl.when(c != zh)(to_sibling.wait_send)

    @pl.when(x != y)
    def _():
        to_pick.wait_send()
        to_diagonal.wait_send()

    @pl.when(picks)
    def _():
        for dy, ds in moves:
            pick(dy, ds).wait_send()


def exchanged(eigvecs, momenta, source_times, perambulator):
    dma = pltpu.SemaphoreType.DMA

    def vmem(*lead, kind=BF16):
        return pltpu.VMEM(lead + (ROWS, COLS), kind)

    return pl.pallas_call(
        exchange,
        out_shape=jax.ShapeDtypeStruct((NY, 2, 2, 4, ROWS, COLS), F32),
        in_specs=[pl.BlockSpec(memory_space=pltpu.HBM)] * 4,
        out_specs=pl.BlockSpec(memory_space=pltpu.VMEM),
        scratch_shapes=[
            vmem(2, 4, 8), vmem(2, 4, 8), pltpu.VMEM((2, COLS, COLS), BF16),
            pltpu.VMEM((2, SITES, COLS), BF16), pltpu.SMEM((NY, 3), jnp.int32), pltpu.SMEM((2,), jnp.int32),
            pltpu.VMEM((SITES, 8), F32), pltpu.VMEM((2, COLS, SITES), BF16), pltpu.VMEM((2, SITES, COLS), BF16),
            pltpu.VMEM((2, SITES, COLS), BF16),
            vmem(4, 8), vmem(4, 8), vmem(4, 8, kind=F32), vmem(3, 8), vmem(3, 8), vmem(8), vmem(8), vmem(2), vmem(4, 2),
            pltpu.VMEM((4, 2, 8, COLS), jnp.int32), vmem(4, 2), vmem(2), vmem(2, 4),
            pltpu.VMEM((2, 2, 4, COLS, COLS), BF16),
            dma((4,)), dma((2, 2)), dma((4,)), dma((4,)), dma, dma((4,)), dma((3,)), dma((3,)), dma((8,)), dma((8,)),
            dma, dma((4,)), dma((4, 2)), dma((2, 4)), dma((4, 2)), dma((2,)),
            dma((8,)), dma((8,)), dma((3, 8)), dma((3, 8)), dma((4, 8)), dma((4, 8)),
        ],
        compiler_params=pltpu.CompilerParams(
            collective_id=0, has_side_effects=True, vmem_limit_bytes=50 * 1024 * 1024
        ),
    )(eigvecs, momenta, source_times, perambulator)


def local(eigvecs, perambulator, momenta, source_times):
    def here(value):
        return pltpu.with_memory_space_constraint(value, pltpu.HBM)

    return exchanged(here(eigvecs), here(momenta), here(source_times), here(perambulator))


def solution(mesh):
    placed = (P("snk", ("src", "slab"), None), P("snk", "src", None, None, None), P(), P("src"))
    return jax.shard_map(
        local,
        mesh=mesh,
        in_specs=placed,
        out_specs=P(None, "snk", "src", None, "slab", None),
        check_vma=False,
    )
```

```python
import math

import jax
import jax.numpy as jnp
from jax import lax
from jax.experimental import pallas as pl
from jax.experimental.pallas import tpu as pltpu
from jax.sharding import PartitionSpec as P

LX = 32
LY = 32
LZ = 32
NX = 4
NY = 4
NZ = 8
ZLO = 4
NEV = 192
COLS = 2 * NEV
SITES = LX * LY
ROWS = 24
MESH = pl.DeviceIdType.MESH
F32 = jnp.float32
BF16 = jnp.bfloat16


def block_of(z):
    return lax.rem(z, ZLO) * 2 + lax.div(z, ZLO)


def turned(columns):
    lane = lax.broadcasted_iota(jnp.int32, columns.shape, 1)
    return pltpu.roll(columns, NEV, 1) * jnp.where(lane < NEV, 1.0, -1.0)


def swap_matrix():
    at_row = lax.broadcasted_iota(jnp.int32, (COLS, COLS), 0)
    at_col = lax.broadcasted_iota(jnp.int32, (COLS, COLS), 1)
    return (jnp.where(at_col == at_row + NEV, 1.0, 0.0) - jnp.where(at_row == at_col + NEV, 1.0, 0.0)).astype(BF16)


def exchange(eigvecs, momenta, source_times, peram, blocks, src, half, both, eig, mom, st, trig, vt, vs, w, dsend, d2d,
             mine, ysend, yrecv, q, zrecv, xall, stall, sel, es, ep, sink, pcat,
             in_s, p_s, d2d_s, d2d_r, st_s, st_r, y_s, y_r, z_s, z_r, x_s, x_r, sel_s, sel_r,
             es_s, es_r, ep_s, ep_r, sink_s, sink_r, up_s, up_r, out_s, out_r, sib_s, sib_r):
    y = lax.axis_index("src")
    snk = lax.axis_index("snk")
    slab = lax.axis_index("slab")
    zh, x = lax.div(snk, NX), lax.rem(snk, NX)
    zl, c = lax.div(slab, 2), lax.rem(slab, 2)
    z = zh * ZLO + zl
    own = block_of(z)
    picks = x == y

    def at(y=y, x=x, z=None, zh=zh, zl=zl, c=c):
        if z is not None:
            zh, zl = lax.div(z, ZLO), lax.rem(z, ZLO)
        return {"src": y, "snk": zh * NX + x, "slab": zl * 2 + c}

    def turn(value, by, size):
        return lax.rem(value + by, size)

    def copy(source, target, send, recv, device):
        return pltpu.make_async_remote_copy(
            src_ref=source, dst_ref=target, send_sem=send, recv_sem=recv, device_id=device, device_id_type=MESH
        )

    fetches = [
        pltpu.make_async_copy(momenta, mom, in_s.at[0]),
        pltpu.make_async_copy(source_times, st, in_s.at[1]),
        pltpu.make_async_copy(eigvecs.at[1 - c], eig.at[1 - c], in_s.at[2]),
        pltpu.make_async_copy(eigvecs.at[c], eig.at[c], in_s.at[3]),
    ]
    loads = []
    for t in range(2):
        for s in range(2):
            loads.append(pltpu.make_async_copy(peram.at[t, s], pcat.at[t, s, :, pl.ds(0, NEV)], p_s.at[t, s]))
    for each in fetches:
        each.start()

    barrier = pltpu.get_barrier_semaphore()
    peers = [at(z=turn(z, k, NZ)) for k in (4, 3, 5)] + [at(x=turn(x, 2, NX), c=k) for k in range(2)]
    peers += [at(y=turn(y, 2, NY))] + [at(z=turn(z, k, NZ)) for k in (2, 6)]
    peers += [at(x=turn(x, d, NX), c=k) for d in (1, 3) for k in range(2)]
    peers += [at(y=turn(y, d, NY)) for d in (1, 3)] + [at(z=turn(z, k, NZ)) for k in (1, 7)] + [at(c=1 - c)]
    for peer in peers:
        pl.semaphore_signal(barrier, inc=1, device_id=peer, device_id_type=MESH)
    fetches[0].wait()
    fetches[2].wait()

    sends = []
    sibling = at(c=1 - c)

    row = lax.broadcasted_iota(jnp.int32, (8, SITES), 0)
    site = lax.broadcasted_iota(jnp.int32, (8, SITES), 1)

    def component(k):
        value = jnp.zeros((8, SITES), jnp.int32)
        for d in range(NY):
            value = jnp.where((row & 3) == d, mom[turn(y, d, NY), k], value)
        return value

    plane = y * NZ + slab
    fx = ((component(0) * (site & (LX - 1))) & (LX - 1)).astype(F32) / LX
    fy = ((component(1) * ((site >> 5) & (LY - 1))) & (LY - 1)).astype(F32) / LY
    fz = ((component(2) * plane) & (LZ - 1)).astype(F32) / LZ
    angle = 2.0 * math.pi * (fx + fy + fz - jnp.where(row < 4, 0.0, 0.25))
    trig[...] = jnp.cos(angle).T

    def prepare(t):
        vt[t] = eig[t].T
        for r in range(0, SITES, 256):
            vs[t, r : r + 256] = -jnp.dot(eig[t, r : r + 256], swap, preferred_element_type=F32).astype(BF16)

    def phase(t, d, slot):
        for r in range(0, SITES, 128):
            cosine = trig[r : r + 128, d : d + 1]
            sine = trig[r : r + 128, d + 4 : d + 5]
            phased = cosine * eig[t, r : r + 128].astype(F32) + sine * vs[t, r : r + 128].astype(F32)
            w[slot, r : r + 128] = phased.astype(BF16)

    swap = swap_matrix()
    prepare(1 - c)

    pair = {}
    along = {}
    turns = ((1, 2), (1, 1), (0, 2), (1, 3), (0, 1), (0, 3), (1, 0), (0, 0))

    def time(other):
        return 1 - c if other else c

    def go_along(d):
        pair[d].wait_recv()
        ysend[d - 1] = (mine[d] + d2d[d].astype(F32)).astype(BF16)
        along[d] = copy(ysend.at[d - 1], yrecv.at[d - 1], y_s.at[d - 1], y_r.at[d - 1], at(y=turn(y, d, NY)))
        along[d].start()

    phase(1 - c, 2, 0)
    for k, (other, d) in enumerate(turns):
        if k == 1:
            fetches[3].wait()
            for each in loads:
                each.start()
            prepare(c)
        if k + 1 < len(turns):
            phase(time(turns[k + 1][0]), turns[k + 1][1], (k + 1) % 2)
        gram = jnp.dot(vt[time(other)], w[k % 2], preferred_element_type=F32)
        value = (gram[:NEV] + turned(gram[NEV:])).reshape(NZ, ROWS, COLS)
        if other:
            dsend[d] = value.astype(BF16)
            pair[d] = copy(dsend.at[d], d2d.at[d], d2d_s.at[d], d2d_r.at[d], sibling)
        else:
            mine[d] = value
        if k == 1:
            pl.semaphore_wait(barrier, len(peers))
            for each in (2, 1):
                pair[each].start()
            fetches[1].wait()
            for s in range(2):
                stall[y, s] = jnp.full((8, COLS), st[s], jnp.int32)
            to_pick = copy(stall.at[y], stall.at[y], st_s, st_r.at[y], at(y=x))
            pl.when(x != y)(to_pick.start)
        elif k and other:
            pair[d].start()
        elif k and d:
            go_along(d)
    along = [along[d] for d in (2, 1, 3)]
    sends += list(pair.values()) + along

    for each in loads:
        each.wait()
    for t in range(2):
        for s in range(2):
            for k in range(4):
                pcat[t, s, k, NEV:] = jnp.dot(pcat[t, s, k, :NEV], swap, preferred_element_type=F32).astype(BF16)

    pair[0].wait_recv()
    for each in along:
        each.wait_recv()

    def summed(block):
        total = mine[0, block] + d2d[0, block].astype(F32)
        for d in range(3):
            total += yrecv[d, block].astype(F32)
        return total.astype(BF16)

    for dz in (4, 3, 5, 2, 6, 1, 7):
        to = turn(z, dz, NZ)
        q[dz] = summed(block_of(to))
        each = copy(q.at[dz], zrecv.at[z], z_s.at[dz], z_r.at[z], at(z=to))
        each.start()
        sends.append(each)
    zrecv[z] = summed(own)
    for dz in range(1, NZ):
        come = turn(z, dz, NZ)
        copy(q.at[dz], zrecv.at[come], z_s.at[dz], z_r.at[come], at(z=come)).wait_recv()
    for g in range(2):
        total = zrecv[g * ZLO].astype(F32)
        for k in range(1, ZLO):
            total += zrecv[g * ZLO + k].astype(F32)
        es[y, g] = total.astype(BF16)

    def to_diagonal(k):
        return copy(es.at[y], xall.at[x, c], x_s.at[k], x_r.at[x, c], at(x=y, c=turn(c, k, 2)))

    @pl.when(x != y)
    def _():
        for k in range(2):
            to_diagonal(k).start()

    for d in (2, 1, 3):
        each = copy(es.at[y], es.at[y], es_s.at[d - 1], es_r.at[y], at(y=turn(y, d, NY)))
        each.start()
        sends.append(each)

    def picked(plane):
        wanted = stall[plane, c][0:1]
        total = jnp.zeros((ROWS, COLS), F32)
        for k in range(NX):
            for parity in range(2):
                for g in range(2):
                    total += jnp.where(wanted == 2 * (g * NX + k) + parity, xall[k, parity, g].astype(F32), 0.0)
        return total.astype(BF16)

    def pick(dy):
        return copy(sel.at[dy], src.at[c, x, 0], sel_s.at[dy], sel_r, at(y=turn(y, dy, NY)))

    @pl.when(picks)
    def _():
        to_diagonal(1).start()
        xall[x, c] = es[y]
        for d in (0, 1, 3, 2):
            for k in range(2):
                if d or k:
                    come, parity = turn(x, d, NX), turn(c, k, 2)
                    copy(es.at[y], xall.at[come, parity], x_s.at[k], x_r.at[come, parity], at(x=come, c=1 - c)).wait_recv()
            if d:
                come = turn(y, d, NY)
                copy(stall.at[come], stall.at[come], st_s, st_r.at[come], at(y=come)).wait_recv()
        for dy in (2, 1, 3):
            sel[dy] = picked(turn(y, dy, NY))
            pick(dy).start()
        src[c, x, 0] = picked(y)

    @pl.when(x != y)
    def _():
        pick(1).wait_recv()

    groups = ((0, 1), (1, 2), (6, 2), (3, 3))

    def piece(s, m, group):
        return src.at[s, m, pl.ds(groups[group][0], groups[group][1])]

    for dz in (1, 7, 2, 6, 3, 5, 4):
        each = copy(src.at[c, x, 0], src.at[c, x, NZ - dz], up_s.at[dz], up_r.at[NZ - dz], at(z=turn(z, dz, NZ)))
        each.start()
        sends.append(each)

    def share(group, d):
        m = turn(x, NX - d, NX)
        each = copy(piece(c, m, group), piece(c, m, group), sib_s.at[d, group], sib_r.at[d, group], sibling)
        each.start()
        sends.append(each)

    def spread(group):
        for d in (2, 1, 3):
            each = copy(piece(c, x, group), piece(c, x, group), out_s.at[d - 1, group], out_r.at[d - 1, group],
                        at(x=turn(x, d, NX)))
            each.start()
            sends.append(each)
        share(group, 0)

    spread(0)

    for d in (1, 2, 3):
        m = turn(y, d, NY)
        copy(es.at[m], es.at[m], es_s.at[d - 1], es_r.at[m], at(y=m)).wait_recv()
    opposite = copy(es.at[:, 1 - zh], ep, ep_s, ep_r, at(z=turn(z, ZLO, NZ)))
    opposite.start()
    sends.append(opposite)

    for group in (1, 2, 3):
        for k in range(groups[group][0], sum(groups[group])):
            copy(src.at[c, x, 0], src.at[c, x, k], up_s.at[1], up_r.at[k], at(z=turn(z, k, NZ))).wait_recv()
        spread(group)

    def come_out(group, d):
        m = turn(x, NX - d, NX)
        copy(piece(c, m, group), piece(c, m, group), out_s.at[d - 1, group], out_r.at[d - 1, group], at(x=m)).wait_recv()

    def come_shared(group, d):
        m = turn(x, NX - d, NX)
        copy(piece(1 - c, m, group), piece(1 - c, m, group), sib_s.at[d, group], sib_r.at[d, group], sibling).wait_recv()

    for d in (1, 3, 2):
        come_out(0, d)
        share(0, d)

    opposite.wait_recv()
    near = copy(ep, sink.at[c], sink_s, sink_r.at[c], sibling)
    far = copy(es.at[:, zh], sink.at[c], sink_s, sink_r.at[c], sibling)

    @pl.when(c == zh)
    def _():
        near.start()
        for m in range(NY):
            sink[c, m] = es[m, zh]

    @pl.when(c != zh)
    def _():
        far.start()
        sink[c] = ep[...]

    sends.append(near)

    for group in (1, 2):
        for d in (1, 3, 2):
            come_out(group, d)
            share(group, d)

    copy(ep, sink.at[1 - c], sink_s, sink_r.at[1 - c], sibling).wait_recv()
    for t in range(2):
        left = sink[t].astype(F32).reshape(NY * ROWS, COLS).astype(BF16)
        for s in range(2):
            for k in range(4):
                value = jnp.dot(left, pcat[t, s, k], preferred_element_type=F32)
                value = value.reshape(NY, ROWS, COLS).astype(BF16)
                for m in range(NY):
                    half[s, m, 4 * t + k] = value[m]


    def flat(value):
        return value.astype(F32).reshape(NEV, COLS).astype(BF16)

    def finish(s, d):
        slot, m = d % 2, turn(x, NX - d, NX)
        heights = [(b % 2) * ZLO + b // 2 for b in range(NZ)]
        rows = [src[s, m, turn(height + NZ, -z, NZ)].astype(F32) for height in heights]
        rows = jnp.concatenate(rows, axis=0).astype(BF16)
        both[slot, :NEV] = rows
        both[slot, NEV:] = jnp.dot(rows, swap, preferred_element_type=F32).astype(BF16)
        value = lax.dot_general(flat(half[s, m]), both[slot], (((1,), (1,)), ((), ())), preferred_element_type=F32)
        value = value.reshape(2, 4, ROWS, COLS)
        for t in range(2):
            blocks[m, t, s] = value[t]

    finish(c, 0)
    for group in range(4):
        come_shared(group, 0)
    finish(1 - c, 0)
    for d in (1, 3, 2):
        come_out(3, d)
        share(3, d)
    for d in (1, 3, 2):
        finish(c, d)
    for d in (1, 3, 2):
        for group in range(4):
            come_shared(group, d)
        finish(1 - c, d)

    for each in sends:
        each.wait_send()

    @pl.when(x != y)
    def _():
        to_pick.wait_send()
        to_diagonal(0).wait_send()

    to_diagonal(1).wait_send()

    @pl.when(picks)
    def _():
        for dy in (2, 1, 3):
            pick(dy).wait_send()


def exchanged(eigvecs, momenta, source_times, perambulator):
    dma = pltpu.SemaphoreType.DMA

    def vmem(*lead, kind=BF16):
        return pltpu.VMEM(lead + (ROWS, COLS), kind)

    return pl.pallas_call(
        exchange,
        out_shape=jax.ShapeDtypeStruct((NY, 2, 2, 4, ROWS, COLS), F32),
        in_specs=[pl.BlockSpec(memory_space=pltpu.HBM)] * 4,
        out_specs=pl.BlockSpec(memory_space=pltpu.VMEM),
        scratch_shapes=[
            vmem(2, 4, 8), vmem(2, 4, 8), pltpu.VMEM((2, COLS, COLS), BF16),
            pltpu.VMEM((2, SITES, COLS), BF16), pltpu.SMEM((NY, 3), jnp.int32), pltpu.SMEM((2,), jnp.int32),
            pltpu.VMEM((SITES, 8), F32), pltpu.VMEM((2, COLS, SITES), BF16), pltpu.VMEM((2, SITES, COLS), BF16),
            pltpu.VMEM((2, SITES, COLS), BF16),
            vmem(4, 8), vmem(4, 8), vmem(4, 8, kind=F32), vmem(3, 8), vmem(3, 8), vmem(8), vmem(8), vmem(4, 2, 2),
            pltpu.VMEM((4, 2, 8, COLS), jnp.int32), vmem(4), vmem(4, 2), vmem(4), vmem(2, 4),
            pltpu.VMEM((2, 2, 4, COLS, COLS), BF16),
            dma((4,)), dma((2, 2)), dma((4,)), dma((4,)), dma, dma((4,)), dma((3,)), dma((3,)), dma((8,)), dma((8,)),
            dma((2,)), dma((4, 2)), dma((4,)), dma,
            dma((3,)), dma((4,)), dma, dma, dma, dma((2,)), dma((8,)), dma((8,)),
            dma((3, 4)), dma((3, 4)), dma((4, 4)), dma((4, 4)),
        ],
        compiler_params=pltpu.CompilerParams(
            collective_id=0, has_side_effects=True, vmem_limit_bytes=50 * 1024 * 1024
        ),
    )(eigvecs, momenta, source_times, perambulator)


def local(eigvecs, perambulator, momenta, source_times):
    def here(value):
        return pltpu.with_memory_space_constraint(value, pltpu.HBM)

    return exchanged(here(eigvecs), here(momenta), here(source_times), here(perambulator))


def solution(mesh):
    placed = (P("snk", ("src", "slab"), None), P("snk", "src", None, None, None), P(), P("src"))
    return jax.shard_map(
        local,
        mesh=mesh,
        in_specs=placed,
        out_specs=P(None, "snk", "src", None, "slab", None),
        check_vma=False,
    )
```

```python
import math

import jax
import jax.numpy as jnp
from jax import lax
from jax.experimental import pallas as pl
from jax.experimental.pallas import tpu as pltpu
from jax.sharding import PartitionSpec as P

LX = 32
LY = 32
LZ = 32
NX = 4
NY = 4
NZ = 8
ZLO = 4
NEV = 192
COLS = 2 * NEV
SITES = LX * LY
ROWS = 24
MESH = pl.DeviceIdType.MESH
F32 = jnp.float32
BF16 = jnp.bfloat16


def block_of(z):
    return lax.rem(z, ZLO) * 2 + lax.div(z, ZLO)


def turned(columns):
    lane = lax.broadcasted_iota(jnp.int32, columns.shape, 1)
    return pltpu.roll(columns, NEV, 1) * jnp.where(lane < NEV, 1.0, -1.0)


def swap_matrix():
    at_row = lax.broadcasted_iota(jnp.int32, (COLS, COLS), 0)
    at_col = lax.broadcasted_iota(jnp.int32, (COLS, COLS), 1)
    return (jnp.where(at_col == at_row + NEV, 1.0, 0.0) - jnp.where(at_row == at_col + NEV, 1.0, 0.0)).astype(BF16)


def exchange(eigvecs, momenta, source_times, peram, blocks, src, half, both, eig, mom, st, trig, vt, vs, w, dsend, d2d,
             mine, ysend, yrecv, q, zrecv, xall, stall, sel, es, ep, sink, pcat,
             in_s, p_s, d2d_s, d2d_r, st_s, st_r, y_s, y_r, z_s, z_r, x_s, x_r, sel_s, sel_r,
             es_s, es_r, ep_s, ep_r, sink_s, sink_r, up_s, up_r, out_s, out_r, sib_s, sib_r):
    y = lax.axis_index("src")
    snk = lax.axis_index("snk")
    slab = lax.axis_index("slab")
    zh, x = lax.div(snk, NX), lax.rem(snk, NX)
    zl, c = lax.div(slab, 2), lax.rem(slab, 2)
    z = zh * ZLO + zl
    picks = x == y

    def at(y=y, x=x, z=None, zh=zh, zl=zl, c=c):
        if z is not None:
            zh, zl = lax.div(z, ZLO), lax.rem(z, ZLO)
        return {"src": y, "snk": zh * NX + x, "slab": zl * 2 + c}

    def turn(value, by, size):
        return lax.rem(value + by, size)

    def copy(source, target, send, recv, device):
        return pltpu.make_async_remote_copy(
            src_ref=source, dst_ref=target, send_sem=send, recv_sem=recv, device_id=device, device_id_type=MESH
        )

    fetches = [
        pltpu.make_async_copy(momenta, mom, in_s.at[0]),
        pltpu.make_async_copy(source_times, st, in_s.at[1]),
        pltpu.make_async_copy(eigvecs.at[1 - c], eig.at[1 - c], in_s.at[2]),
        pltpu.make_async_copy(eigvecs.at[c], eig.at[c], in_s.at[3]),
    ]
    loads = []
    for t in range(2):
        for s in range(2):
            loads.append(pltpu.make_async_copy(peram.at[t, s], pcat.at[t, s, :, pl.ds(0, NEV)], p_s.at[t, s]))
    for each in fetches:
        each.start()

    barrier = pltpu.get_barrier_semaphore()
    peers = [at(z=turn(z, k, NZ)) for k in (4, 3, 5)] + [at(x=turn(x, 2, NX), c=k) for k in range(2)]
    peers += [at(y=turn(y, 2, NY))] + [at(z=turn(z, k, NZ)) for k in (2, 6)]
    peers += [at(x=turn(x, d, NX), c=k) for d in (1, 3) for k in range(2)]
    peers += [at(y=turn(y, d, NY)) for d in (1, 3)] + [at(z=turn(z, k, NZ)) for k in (1, 7)] + [at(c=1 - c)]
    for peer in peers:
        pl.semaphore_signal(barrier, inc=1, device_id=peer, device_id_type=MESH)
    fetches[0].wait()
    fetches[2].wait()

    sends = []
    sibling = at(c=1 - c)

    row = lax.broadcasted_iota(jnp.int32, (8, SITES), 0)
    site = lax.broadcasted_iota(jnp.int32, (8, SITES), 1)

    def component(k):
        value = jnp.zeros((8, SITES), jnp.int32)
        for d in range(NY):
            value = jnp.where((row & 3) == d, mom[turn(y, d, NY), k], value)
        return value

    plane = y * NZ + slab
    fx = ((component(0) * (site & (LX - 1))) & (LX - 1)).astype(F32) / LX
    fy = ((component(1) * ((site >> 5) & (LY - 1))) & (LY - 1)).astype(F32) / LY
    fz = ((component(2) * plane) & (LZ - 1)).astype(F32) / LZ
    angle = 2.0 * math.pi * (fx + fy + fz - jnp.where(row < 4, 0.0, 0.25))
    trig[...] = jnp.cos(angle).T

    def prepare(t):
        vt[t] = eig[t].T
        for r in range(0, SITES, 256):
            vs[t, r : r + 256] = -jnp.dot(eig[t, r : r + 256], swap, preferred_element_type=F32).astype(BF16)

    def phase(t, d, slot):
        for r in range(0, SITES, 128):
            cosine = trig[r : r + 128, d : d + 1]
            sine = trig[r : r + 128, d + 4 : d + 5]
            phased = cosine * eig[t, r : r + 128].astype(F32) + sine * vs[t, r : r + 128].astype(F32)
            w[slot, r : r + 128] = phased.astype(BF16)

    swap = swap_matrix()
    prepare(1 - c)

    pair = {}
    along = {}
    turns = ((1, 2), (1, 1), (0, 2), (1, 3), (0, 1), (0, 3), (1, 0), (0, 0))

    def time(other):
        return 1 - c if other else c

    slots = [turn((b % 2) * ZLO + b // 2 + 2 * NZ - 2, -z, NZ) for b in range(NZ)]

    def ready(d):
        pair[d].wait_recv()
        for b in range(NZ):
            ysend[d - 1, slots[b]] = (mine[d, b] + d2d[d, b].astype(F32)).astype(BF16)

    def go_along(d, part):
        there = pl.ds(4 * part, 4)
        along[d, part] = copy(ysend.at[d - 1, there], yrecv.at[d - 1, there], y_s.at[d - 1, part],
                              y_r.at[d - 1, part], at(y=turn(y, d, NY)))
        along[d, part].start()

    after = {2: ((2, 0),), 1: ((1, 0), (2, 1)), 3: ((3, 0), (1, 1), (3, 1))}
    phase(1 - c, 2, 0)
    for k, (other, d) in enumerate(turns):
        if k == 1:
            fetches[3].wait()
            for each in loads:
                each.start()
            prepare(c)
        if k + 1 < len(turns):
            phase(time(turns[k + 1][0]), turns[k + 1][1], (k + 1) % 2)
        gram = jnp.dot(vt[time(other)], w[k % 2], preferred_element_type=F32)
        value = (gram[:NEV] + turned(gram[NEV:])).reshape(NZ, ROWS, COLS)
        if other:
            dsend[d] = value.astype(BF16)
            pair[d] = copy(dsend.at[d], d2d.at[d], d2d_s.at[d], d2d_r.at[d], sibling)
        else:
            mine[d] = value
        if k == 1:
            pl.semaphore_wait(barrier, len(peers))
            for each in (2, 1):
                pair[each].start()
            fetches[1].wait()
            for s in range(2):
                stall[y, s] = jnp.full((8, COLS), st[s], jnp.int32)
            to_pick = copy(stall.at[y], stall.at[y], st_s, st_r.at[y], at(y=x))
            pl.when(x != y)(to_pick.start)
        elif k and other:
            pair[d].start()
        elif k and d:
            ready(d)
            for each in after[d]:
                go_along(*each)
    sends += list(pair.values()) + list(along.values())

    for each in loads:
        each.wait()
    for t in range(2):
        for s in range(2):
            for k in range(4):
                pcat[t, s, k, NEV:] = jnp.dot(pcat[t, s, k, :NEV], swap, preferred_element_type=F32).astype(BF16)

    pair[0].wait_recv()

    def summed(r):
        block = block_of(turn(z, r, NZ))
        total = mine[0, block] + d2d[0, block].astype(F32)
        for d in range(3):
            total += yrecv[d, (r + 6) % NZ].astype(F32)
        return total.astype(BF16)

    for part, heights in ((0, (4, 3, 5, 2)), (1, (6, 1, 7))):
        for d in (2, 1, 3):
            along[d, part].wait_recv()
        for dz in heights:
            q[dz] = summed(dz)
            each = copy(q.at[dz], zrecv.at[z], z_s.at[dz], z_r.at[z], at(z=turn(z, dz, NZ)))
            each.start()
            sends.append(each)
    zrecv[z] = summed(0)
    for dz in range(1, NZ):
        come = turn(z, dz, NZ)
        copy(q.at[dz], zrecv.at[come], z_s.at[dz], z_r.at[come], at(z=come)).wait_recv()
    for g in range(2):
        total = zrecv[g * ZLO].astype(F32)
        for k in range(1, ZLO):
            total += zrecv[g * ZLO + k].astype(F32)
        es[y, g] = total.astype(BF16)

    def to_diagonal(k):
        return copy(es.at[y], xall.at[x, c], x_s.at[k], x_r.at[x, c], at(x=y, c=turn(c, k, 2)))

    @pl.when(x != y)
    def _():
        for k in range(2):
            to_diagonal(k).start()

    for d in (2, 1, 3):
        each = copy(es.at[y], es.at[y], es_s.at[d - 1], es_r.at[y], at(y=turn(y, d, NY)))
        each.start()
        sends.append(each)

    def picked(plane):
        wanted = stall[plane, c][0:1]
        total = jnp.zeros((ROWS, COLS), F32)
        for k in range(NX):
            for parity in range(2):
                for g in range(2):
                    total += jnp.where(wanted == 2 * (g * NX + k) + parity, xall[k, parity, g].astype(F32), 0.0)
        return total.astype(BF16)

    def pick(dy):
        return copy(sel.at[dy], src.at[c, x, 0], sel_s.at[dy], sel_r, at(y=turn(y, dy, NY)))

    @pl.when(picks)
    def _():
        to_diagonal(1).start()
        xall[x, c] = es[y]
        for d in (0, 1, 3, 2):
            for k in range(2):
                if d or k:
                    come, parity = turn(x, d, NX), turn(c, k, 2)
                    copy(es.at[y], xall.at[come, parity], x_s.at[k], x_r.at[come, parity], at(x=come, c=1 - c)).wait_recv()
            if d:
                come = turn(y, d, NY)
                copy(stall.at[come], stall.at[come], st_s, st_r.at[come], at(y=come)).wait_recv()
        for dy in (2, 1, 3):
            sel[dy] = picked(turn(y, dy, NY))
            pick(dy).start()
        src[c, x, 0] = picked(y)

    for d in (1, 2, 3):
        m = turn(y, d, NY)
        copy(es.at[m], es.at[m], es_s.at[d - 1], es_r.at[m], at(y=m)).wait_recv()
    opposite = copy(es.at[:, 1 - zh], ep, ep_s, ep_r, at(z=turn(z, ZLO, NZ)))
    opposite.start()
    sends.append(opposite)

    @pl.when(x != y)
    def _():
        pick(1).wait_recv()

    groups = ((0, 1), (1, 2), (6, 2), (3, 3))

    def piece(s, m, group):
        return src.at[s, m, pl.ds(groups[group][0], groups[group][1])]

    for dz in (1, 7, 2, 6, 3, 5, 4):
        each = copy(src.at[c, x, 0], src.at[c, x, NZ - dz], up_s.at[dz], up_r.at[NZ - dz], at(z=turn(z, dz, NZ)))
        each.start()
        sends.append(each)

    def share(group, d):
        m = turn(x, NX - d, NX)
        each = copy(piece(c, m, group), piece(c, m, group), sib_s.at[d, group], sib_r.at[d, group], sibling)
        each.start()
        sends.append(each)

    def spread(group):
        for d in (2, 1, 3):
            each = copy(piece(c, x, group), piece(c, x, group), out_s.at[d - 1, group], out_r.at[d - 1, group],
                        at(x=turn(x, d, NX)))
            each.start()
            sends.append(each)
        share(group, 0)

    spread(0)

    def come_up(group):
        for k in range(groups[group][0], sum(groups[group])):
            copy(src.at[c, x, 0], src.at[c, x, k], up_s.at[1], up_r.at[k], at(z=turn(z, k, NZ))).wait_recv()
        spread(group)

    def come_out(group, d):
        m = turn(x, NX - d, NX)
        copy(piece(c, m, group), piece(c, m, group), out_s.at[d - 1, group], out_r.at[d - 1, group], at(x=m)).wait_recv()

    def come_shared(group, d):
        m = turn(x, NX - d, NX)
        copy(piece(1 - c, m, group), piece(1 - c, m, group), sib_s.at[d, group], sib_r.at[d, group], sibling).wait_recv()

    opposite.wait_recv()
    near = copy(ep, sink.at[c], sink_s, sink_r.at[c], sibling)
    far = copy(es.at[:, zh], sink.at[c], sink_s, sink_r.at[c], sibling)

    @pl.when(c == zh)
    def _():
        near.start()
        for m in range(NY):
            sink[c, m] = es[m, zh]

    @pl.when(c != zh)
    def _():
        far.start()
        sink[c] = ep[...]

    sends.append(near)
    come_up(1)
    come_up(2)

    copy(ep, sink.at[1 - c], sink_s, sink_r.at[1 - c], sibling).wait_recv()
    for t in range(2):
        left = sink[t].astype(F32).reshape(NY * ROWS, COLS).astype(BF16)
        for s in range(2):
            for k in range(4):
                value = jnp.dot(left, pcat[t, s, k], preferred_element_type=F32)
                value = value.reshape(NY, ROWS, COLS).astype(BF16)
                for m in range(NY):
                    half[s, m, 4 * t + k] = value[m]

    come_up(3)
    for group in (0, 1, 2):
        for d in (1, 3, 2):
            come_out(group, d)
            share(group, d)


    def flat(value):
        return value.astype(F32).reshape(NEV, COLS).astype(BF16)

    def finish(s, d):
        slot, m = d % 2, turn(x, NX - d, NX)
        heights = [(b % 2) * ZLO + b // 2 for b in range(NZ)]
        rows = [src[s, m, turn(height + NZ, -z, NZ)].astype(F32) for height in heights]
        rows = jnp.concatenate(rows, axis=0).astype(BF16)
        both[slot, :NEV] = rows
        both[slot, NEV:] = jnp.dot(rows, swap, preferred_element_type=F32).astype(BF16)
        value = lax.dot_general(flat(half[s, m]), both[slot], (((1,), (1,)), ((), ())), preferred_element_type=F32)
        value = value.reshape(2, 4, ROWS, COLS)
        for t in range(2):
            blocks[m, t, s] = value[t]

    finish(c, 0)
    for group in range(4):
        come_shared(group, 0)
    finish(1 - c, 0)
    for d in (1, 3, 2):
        come_out(3, d)
        share(3, d)
    for d in (1, 3, 2):
        finish(c, d)
    for d in (1, 3, 2):
        for group in range(4):
            come_shared(group, d)
        finish(1 - c, d)

    for each in sends:
        each.wait_send()

    @pl.when(x != y)
    def _():
        to_pick.wait_send()
        to_diagonal(0).wait_send()

    to_diagonal(1).wait_send()

    @pl.when(picks)
    def _():
        for dy in (2, 1, 3):
            pick(dy).wait_send()


def exchanged(eigvecs, momenta, source_times, perambulator):
    dma = pltpu.SemaphoreType.DMA

    def vmem(*lead, kind=BF16):
        return pltpu.VMEM(lead + (ROWS, COLS), kind)

    return pl.pallas_call(
        exchange,
        out_shape=jax.ShapeDtypeStruct((NY, 2, 2, 4, ROWS, COLS), F32),
        in_specs=[pl.BlockSpec(memory_space=pltpu.HBM)] * 4,
        out_specs=pl.BlockSpec(memory_space=pltpu.VMEM),
        scratch_shapes=[
            vmem(2, 4, 8), vmem(2, 4, 8), pltpu.VMEM((2, COLS, COLS), BF16),
            pltpu.VMEM((2, SITES, COLS), BF16), pltpu.SMEM((NY, 3), jnp.int32), pltpu.SMEM((2,), jnp.int32),
            pltpu.VMEM((SITES, 8), F32), pltpu.VMEM((2, COLS, SITES), BF16), pltpu.VMEM((2, SITES, COLS), BF16),
            pltpu.VMEM((2, SITES, COLS), BF16),
            vmem(4, 8), vmem(4, 8), vmem(4, 8, kind=F32), vmem(3, 8), vmem(3, 8), vmem(8), vmem(8), vmem(4, 2, 2),
            pltpu.VMEM((4, 2, 8, COLS), jnp.int32), vmem(4), vmem(4, 2), vmem(4), vmem(2, 4),
            pltpu.VMEM((2, 2, 4, COLS, COLS), BF16),
            dma((4,)), dma((2, 2)), dma((4,)), dma((4,)), dma, dma((4,)), dma((3, 2)), dma((3, 2)), dma((8,)), dma((8,)),
            dma((2,)), dma((4, 2)), dma((4,)), dma,
            dma((3,)), dma((4,)), dma, dma, dma, dma((2,)), dma((8,)), dma((8,)),
            dma((3, 4)), dma((3, 4)), dma((4, 4)), dma((4, 4)),
        ],
        compiler_params=pltpu.CompilerParams(
            collective_id=0, has_side_effects=True, vmem_limit_bytes=50 * 1024 * 1024
        ),
    )(eigvecs, momenta, source_times, perambulator)


def local(eigvecs, perambulator, momenta, source_times):
    def here(value):
        return pltpu.with_memory_space_constraint(value, pltpu.HBM)

    return exchanged(here(eigvecs), here(momenta), here(source_times), here(perambulator))


def solution(mesh):
    placed = (P("snk", ("src", "slab"), None), P("snk", "src", None, None, None), P(), P("src"))
    return jax.shard_map(
        local,
        mesh=mesh,
        in_specs=placed,
        out_specs=P(None, "snk", "src", None, "slab", None),
        check_vma=False,
    )
```

```python
import math

import jax
import jax.numpy as jnp
from jax import lax
from jax.experimental import pallas as pl
from jax.experimental.pallas import tpu as pltpu
from jax.sharding import PartitionSpec as P

LX = 32
LY = 32
LZ = 32
NX = 4
NY = 4
NZ = 8
ZLO = 4
NEV = 192
COLS = 2 * NEV
SITES = LX * LY
ROWS = 24
MESH = pl.DeviceIdType.MESH
F32 = jnp.float32
BF16 = jnp.bfloat16


def block_of(z):
    return lax.rem(z, ZLO) * 2 + lax.div(z, ZLO)


def turned(columns):
    lane = lax.broadcasted_iota(jnp.int32, columns.shape, 1)
    return pltpu.roll(columns, NEV, 1) * jnp.where(lane < NEV, 1.0, -1.0)


def swap_matrix():
    at_row = lax.broadcasted_iota(jnp.int32, (COLS, COLS), 0)
    at_col = lax.broadcasted_iota(jnp.int32, (COLS, COLS), 1)
    return (jnp.where(at_col == at_row + NEV, 1.0, 0.0) - jnp.where(at_row == at_col + NEV, 1.0, 0.0)).astype(BF16)


def exchange(eigvecs, momenta, source_times, peram, blocks, src, half, both, eig, mom, st, trig, vt, vs, w, dsend, d2d,
             mine, ysend, yrecv, q, zrecv, xall, stall, sel, es, ep, sink, pcat,
             in_s, p_s, d2d_s, d2d_r, st_s, st_r, y_s, y_r, z_s, z_r, x_s, x_r, sel_s, sel_r,
             es_s, es_r, ep_s, ep_r, sink_s, sink_r, up_s, up_r, out_s, out_r, sib_s, sib_r, known):
    y = lax.axis_index("src")
    snk = lax.axis_index("snk")
    slab = lax.axis_index("slab")
    zh, x = lax.div(snk, NX), lax.rem(snk, NX)
    zl, c = lax.div(slab, 2), lax.rem(slab, 2)
    z = zh * ZLO + zl
    picks = x == y

    def at(y=y, x=x, z=None, zh=zh, zl=zl, c=c):
        if z is not None:
            zh, zl = lax.div(z, ZLO), lax.rem(z, ZLO)
        return {"src": y, "snk": zh * NX + x, "slab": zl * 2 + c}

    def turn(value, by, size):
        return lax.rem(value + by, size)

    def copy(source, target, send, recv, device):
        return pltpu.make_async_remote_copy(
            src_ref=source, dst_ref=target, send_sem=send, recv_sem=recv, device_id=device, device_id_type=MESH
        )

    fetches = [
        pltpu.make_async_copy(momenta, mom, in_s.at[0]),
        pltpu.make_async_copy(source_times, st, in_s.at[1]),
        pltpu.make_async_copy(eigvecs.at[1 - c], eig.at[1 - c], in_s.at[2]),
        pltpu.make_async_copy(eigvecs.at[c], eig.at[c], in_s.at[3]),
    ]
    loads = []
    for t in range(2):
        for s in range(2):
            loads.append(pltpu.make_async_copy(peram.at[t, s], pcat.at[t, s, :, pl.ds(0, NEV)], p_s.at[t, s]))
    for each in fetches:
        each.start()

    barrier = pltpu.get_barrier_semaphore()
    peers = [at(y=turn(y, d, NY)) for d in (2, 1, 3)] + [at(z=turn(z, k, NZ)) for k in (1, 7)]
    peers += [at(x=turn(x, d, NX)) for d in (1, 3)] + [at(c=1 - c)]
    for peer in peers:
        pl.semaphore_signal(barrier, inc=1, device_id=peer, device_id_type=MESH)

    def tell(round, height):
        for peer in [at(z=turn(z, k, NZ)) for k in (height, NZ - height)] + [at(x=turn(x, d, NX)) for d in (1, 3)]:
            pl.semaphore_signal(known.at[round], inc=1, device_id=peer, device_id_type=MESH)

    fetches[0].wait()
    fetches[2].wait()

    sends = []
    sibling = at(c=1 - c)

    row = lax.broadcasted_iota(jnp.int32, (8, SITES), 0)
    site = lax.broadcasted_iota(jnp.int32, (8, SITES), 1)

    def component(k):
        value = jnp.zeros((8, SITES), jnp.int32)
        for d in range(NY):
            value = jnp.where((row & 3) == d, mom[turn(y, d, NY), k], value)
        return value

    plane = y * NZ + slab
    fx = ((component(0) * (site & (LX - 1))) & (LX - 1)).astype(F32) / LX
    fy = ((component(1) * ((site >> 5) & (LY - 1))) & (LY - 1)).astype(F32) / LY
    fz = ((component(2) * plane) & (LZ - 1)).astype(F32) / LZ
    angle = 2.0 * math.pi * (fx + fy + fz - jnp.where(row < 4, 0.0, 0.25))
    trig[...] = jnp.cos(angle).T

    def prepare(t):
        vt[t] = eig[t].T
        for r in range(0, SITES, 256):
            vs[t, r : r + 256] = -jnp.dot(eig[t, r : r + 256], swap, preferred_element_type=F32).astype(BF16)

    def phase(t, d, slot):
        for r in range(0, SITES, 128):
            cosine = trig[r : r + 128, d : d + 1]
            sine = trig[r : r + 128, d + 4 : d + 5]
            phased = cosine * eig[t, r : r + 128].astype(F32) + sine * vs[t, r : r + 128].astype(F32)
            w[slot, r : r + 128] = phased.astype(BF16)

    swap = swap_matrix()
    prepare(1 - c)

    pair = {}
    along = {}
    turns = ((1, 2), (1, 1), (0, 2), (1, 3), (0, 1), (0, 3), (1, 0), (0, 0))

    def time(other):
        return 1 - c if other else c

    slots = [turn((b % 2) * ZLO + b // 2 + 2 * NZ - 2, -z, NZ) for b in range(NZ)]

    def ready(d):
        pair[d].wait_recv()
        for b in range(NZ):
            ysend[d - 1, slots[b]] = (mine[d, b] + d2d[d, b].astype(F32)).astype(BF16)

    def go_along(d, part):
        there = pl.ds(4 * part, 4)
        along[d, part] = copy(ysend.at[d - 1, there], yrecv.at[d - 1, there], y_s.at[d - 1, part],
                              y_r.at[d - 1, part], at(y=turn(y, d, NY)))
        along[d, part].start()

    phase(1 - c, 2, 0)
    for k, (other, d) in enumerate(turns):
        if k == 1:
            fetches[3].wait()
            for each in loads:
                each.start()
            prepare(c)
        if k + 1 < len(turns):
            phase(time(turns[k + 1][0]), turns[k + 1][1], (k + 1) % 2)
        gram = jnp.dot(vt[time(other)], w[k % 2], preferred_element_type=F32)
        value = (gram[:NEV] + turned(gram[NEV:])).reshape(NZ, ROWS, COLS)
        if other:
            dsend[d] = value.astype(BF16)
            pair[d] = copy(dsend.at[d], d2d.at[d], d2d_s.at[d], d2d_r.at[d], sibling)
        else:
            mine[d] = value
        if k == 3:
            pl.semaphore_wait(barrier, len(peers))
            for each in (2, 1, 3):
                pair[each].start()
            tell(0, 1)
            fetches[1].wait()
            for s in range(2):
                stall[y, s] = jnp.full((8, COLS), st[s], jnp.int32)
            to_pick = copy(stall.at[y], stall.at[y], st_s, st_r.at[y], at(y=x))
            pl.when(x != y)(to_pick.start)
        if k == 4:
            ready(2)
            go_along(2, 0)
            ready(1)
            go_along(1, 0)
            go_along(2, 1)
        if k == 5:
            ready(3)
            for each in ((3, 0), (1, 1), (3, 1)):
                go_along(*each)
            pl.semaphore_wait(known.at[0], 4)
            tell(1, 2)
        if k == 6:
            pair[0].start()
    sends += list(pair.values()) + list(along.values())

    for each in loads:
        each.wait()
    for t in range(2):
        for s in range(2):
            for k in range(4):
                pcat[t, s, k, NEV:] = jnp.dot(pcat[t, s, k, :NEV], swap, preferred_element_type=F32).astype(BF16)

    pair[0].wait_recv()
    pl.semaphore_wait(known.at[1], 4)

    def summed(r):
        block = block_of(turn(z, r, NZ))
        total = mine[0, block] + d2d[0, block].astype(F32)
        for d in range(3):
            total += yrecv[d, (r + 6) % NZ].astype(F32)
        return total.astype(BF16)

    for part, heights in ((0, (4, 3, 5, 2)), (1, (6, 1, 7))):
        for d in (2, 1, 3):
            along[d, part].wait_recv()
        for dz in heights:
            q[dz] = summed(dz)
            each = copy(q.at[dz], zrecv.at[z], z_s.at[dz], z_r.at[z], at(z=turn(z, dz, NZ)))
            each.start()
            sends.append(each)
    zrecv[z] = summed(0)
    for dz in range(1, NZ):
        come = turn(z, dz, NZ)
        copy(q.at[dz], zrecv.at[come], z_s.at[dz], z_r.at[come], at(z=come)).wait_recv()
    for g in range(2):
        total = zrecv[g * ZLO].astype(F32)
        for k in range(1, ZLO):
            total += zrecv[g * ZLO + k].astype(F32)
        es[y, g] = total.astype(BF16)

    def to_diagonal(k):
        return copy(es.at[y], xall.at[x, c], x_s.at[k], x_r.at[x, c], at(x=y, c=turn(c, k, 2)))

    @pl.when(x != y)
    def _():
        for k in range(2):
            to_diagonal(k).start()

    for d in (2, 1, 3):
        each = copy(es.at[y], es.at[y], es_s.at[d - 1], es_r.at[y], at(y=turn(y, d, NY)))
        each.start()
        sends.append(each)

    def picked(plane):
        wanted = stall[plane, c][0:1]
        total = jnp.zeros((ROWS, COLS), F32)
        for k in range(NX):
            for parity in range(2):
                for g in range(2):
                    total += jnp.where(wanted == 2 * (g * NX + k) + parity, xall[k, parity, g].astype(F32), 0.0)
        return total.astype(BF16)

    def pick(dy):
        return copy(sel.at[dy], src.at[c, x, 0], sel_s.at[dy], sel_r, at(y=turn(y, dy, NY)))

    @pl.when(picks)
    def _():
        to_diagonal(1).start()
        xall[x, c] = es[y]
        for d in (0, 1, 3, 2):
            for k in range(2):
                if d or k:
                    come, parity = turn(x, d, NX), turn(c, k, 2)
                    copy(es.at[y], xall.at[come, parity], x_s.at[k], x_r.at[come, parity], at(x=come, c=1 - c)).wait_recv()
            if d:
                come = turn(y, d, NY)
                copy(stall.at[come], stall.at[come], st_s, st_r.at[come], at(y=come)).wait_recv()
        for dy in (2, 1, 3):
            sel[dy] = picked(turn(y, dy, NY))
            pick(dy).start()
        src[c, x, 0] = picked(y)

    for d in (1, 2, 3):
        m = turn(y, d, NY)
        copy(es.at[m], es.at[m], es_s.at[d - 1], es_r.at[m], at(y=m)).wait_recv()
    opposite = copy(es.at[:, 1 - zh], ep, ep_s, ep_r, at(z=turn(z, ZLO, NZ)))
    opposite.start()
    sends.append(opposite)

    @pl.when(x != y)
    def _():
        pick(1).wait_recv()

    groups = ((0, 1), (1, 2), (6, 2), (3, 3))

    def piece(s, m, group):
        return src.at[s, m, pl.ds(groups[group][0], groups[group][1])]

    for dz in (1, 7, 2, 6, 3, 5, 4):
        each = copy(src.at[c, x, 0], src.at[c, x, NZ - dz], up_s.at[dz], up_r.at[NZ - dz], at(z=turn(z, dz, NZ)))
        each.start()
        sends.append(each)

    def share(group, d):
        m = turn(x, NX - d, NX)
        each = copy(piece(c, m, group), piece(c, m, group), sib_s.at[d, group], sib_r.at[d, group], sibling)
        each.start()
        sends.append(each)

    def spread(group):
        for d in (2, 1, 3):
            each = copy(piece(c, x, group), piece(c, x, group), out_s.at[d - 1, group], out_r.at[d - 1, group],
                        at(x=turn(x, d, NX)))
            each.start()
            sends.append(each)
        share(group, 0)

    spread(0)

    def come_up(group):
        for k in range(groups[group][0], sum(groups[group])):
            copy(src.at[c, x, 0], src.at[c, x, k], up_s.at[1], up_r.at[k], at(z=turn(z, k, NZ))).wait_recv()
        spread(group)

    def come_out(group, d):
        m = turn(x, NX - d, NX)
        copy(piece(c, m, group), piece(c, m, group), out_s.at[d - 1, group], out_r.at[d - 1, group], at(x=m)).wait_recv()

    def come_shared(group, d):
        m = turn(x, NX - d, NX)
        copy(piece(1 - c, m, group), piece(1 - c, m, group), sib_s.at[d, group], sib_r.at[d, group], sibling).wait_recv()

    opposite.wait_recv()
    near = copy(ep, sink.at[c], sink_s, sink_r.at[c], sibling)
    far = copy(es.at[:, zh], sink.at[c], sink_s, sink_r.at[c], sibling)

    @pl.when(c == zh)
    def _():
        near.start()
        for m in range(NY):
            sink[c, m] = es[m, zh]

    @pl.when(c != zh)
    def _():
        far.start()
        sink[c] = ep[...]

    sends.append(near)
    come_up(1)
    come_up(2)

    copy(ep, sink.at[1 - c], sink_s, sink_r.at[1 - c], sibling).wait_recv()
    for t in range(2):
        left = sink[t].astype(F32).reshape(NY * ROWS, COLS).astype(BF16)
        for s in range(2):
            for k in range(4):
                value = jnp.dot(left, pcat[t, s, k], preferred_element_type=F32)
                value = value.reshape(NY, ROWS, COLS).astype(BF16)
                for m in range(NY):
                    half[s, m, 4 * t + k] = value[m]

    come_up(3)
    for group in (0, 1, 2):
        for d in (1, 3, 2):
            come_out(group, d)
            share(group, d)


    def flat(value):
        return value.astype(F32).reshape(NEV, COLS).astype(BF16)

    def finish(s, d):
        slot, m = d % 2, turn(x, NX - d, NX)
        heights = [(b % 2) * ZLO + b // 2 for b in range(NZ)]
        rows = [src[s, m, turn(height + NZ, -z, NZ)].astype(F32) for height in heights]
        rows = jnp.concatenate(rows, axis=0).astype(BF16)
        both[slot, :NEV] = rows
        both[slot, NEV:] = jnp.dot(rows, swap, preferred_element_type=F32).astype(BF16)
        value = lax.dot_general(flat(half[s, m]), both[slot], (((1,), (1,)), ((), ())), preferred_element_type=F32)
        value = value.reshape(2, 4, ROWS, COLS)
        for t in range(2):
            blocks[m, t, s] = value[t]

    finish(c, 0)
    for group in range(4):
        come_shared(group, 0)
    finish(1 - c, 0)
    for d in (1, 3, 2):
        come_out(3, d)
        share(3, d)
    for d in (1, 3, 2):
        finish(c, d)
    for d in (1, 3, 2):
        for group in range(4):
            come_shared(group, d)
        finish(1 - c, d)

    for each in sends:
        each.wait_send()

    @pl.when(x != y)
    def _():
        to_pick.wait_send()
        to_diagonal(0).wait_send()

    to_diagonal(1).wait_send()

    @pl.when(picks)
    def _():
        for dy in (2, 1, 3):
            pick(dy).wait_send()


def exchanged(eigvecs, momenta, source_times, perambulator):
    dma = pltpu.SemaphoreType.DMA

    def vmem(*lead, kind=BF16):
        return pltpu.VMEM(lead + (ROWS, COLS), kind)

    return pl.pallas_call(
        exchange,
        out_shape=jax.ShapeDtypeStruct((NY, 2, 2, 4, ROWS, COLS), F32),
        in_specs=[pl.BlockSpec(memory_space=pltpu.HBM)] * 4,
        out_specs=pl.BlockSpec(memory_space=pltpu.VMEM),
        scratch_shapes=[
            vmem(2, 4, 8), vmem(2, 4, 8), pltpu.VMEM((2, COLS, COLS), BF16),
            pltpu.VMEM((2, SITES, COLS), BF16), pltpu.SMEM((NY, 3), jnp.int32), pltpu.SMEM((2,), jnp.int32),
            pltpu.VMEM((SITES, 8), F32), pltpu.VMEM((2, COLS, SITES), BF16), pltpu.VMEM((2, SITES, COLS), BF16),
            pltpu.VMEM((2, SITES, COLS), BF16),
            vmem(4, 8), vmem(4, 8), vmem(4, 8, kind=F32), vmem(3, 8), vmem(3, 8), vmem(8), vmem(8), vmem(4, 2, 2),
            pltpu.VMEM((4, 2, 8, COLS), jnp.int32), vmem(4), vmem(4, 2), vmem(4), vmem(2, 4),
            pltpu.VMEM((2, 2, 4, COLS, COLS), BF16),
            dma((4,)), dma((2, 2)), dma((4,)), dma((4,)), dma, dma((4,)), dma((3, 2)), dma((3, 2)), dma((8,)), dma((8,)),
            dma((2,)), dma((4, 2)), dma((4,)), dma,
            dma((3,)), dma((4,)), dma, dma, dma, dma((2,)), dma((8,)), dma((8,)),
            dma((3, 4)), dma((3, 4)), dma((4, 4)), dma((4, 4)), pltpu.SemaphoreType.REGULAR((2,)),
        ],
        compiler_params=pltpu.CompilerParams(
            collective_id=0, has_side_effects=True, vmem_limit_bytes=50 * 1024 * 1024
        ),
    )(eigvecs, momenta, source_times, perambulator)


def local(eigvecs, perambulator, momenta, source_times):
    def here(value):
        return pltpu.with_memory_space_constraint(value, pltpu.HBM)

    return exchanged(here(eigvecs), here(momenta), here(source_times), here(perambulator))


def solution(mesh):
    placed = (P("snk", ("src", "slab"), None), P("snk", "src", None, None, None), P(), P("src"))
    return jax.shard_map(
        local,
        mesh=mesh,
        in_specs=placed,
        out_specs=P(None, "snk", "src", None, "slab", None),
        check_vma=False,
    )
```

```python
import math

import jax
import jax.numpy as jnp
from jax import lax
from jax.experimental import pallas as pl
from jax.experimental.pallas import tpu as pltpu
from jax.sharding import PartitionSpec as P

LX = 32
LY = 32
LZ = 32
NX = 4
NY = 4
NZ = 8
ZLO = 4
NEV = 192
COLS = 2 * NEV
SITES = LX * LY
ROWS = 24
MESH = pl.DeviceIdType.MESH
F32 = jnp.float32
BF16 = jnp.bfloat16


def block_of(z):
    return lax.rem(z, ZLO) * 2 + lax.div(z, ZLO)


def turned(columns):
    lane = lax.broadcasted_iota(jnp.int32, columns.shape, 1)
    return pltpu.roll(columns, NEV, 1) * jnp.where(lane < NEV, 1.0, -1.0)


def swap_matrix():
    at_row = lax.broadcasted_iota(jnp.int32, (COLS, COLS), 0)
    at_col = lax.broadcasted_iota(jnp.int32, (COLS, COLS), 1)
    return (jnp.where(at_col == at_row + NEV, 1.0, 0.0) - jnp.where(at_row == at_col + NEV, 1.0, 0.0)).astype(BF16)


def exchange(eigvecs, momenta, source_times, peram, blocks, src, half, both, eig, mom, st, trig, vt, vs, w, dsend, d2d,
             mine, ysend, yrecv, q, zrecv, wanted, sel, srecv, es, ep, sink, pcat,
             in_s, p_s, d2d_s, d2d_r, y_s, y_r, z_s, z_r, sel_s, sel_r,
             es_s, es_r, ep_s, ep_r, sink_s, sink_r, up_s, up_r, out_s, out_r, sib_s, sib_r, known):
    y = lax.axis_index("src")
    snk = lax.axis_index("snk")
    slab = lax.axis_index("slab")
    zh, x = lax.div(snk, NX), lax.rem(snk, NX)
    zl, c = lax.div(slab, 2), lax.rem(slab, 2)
    z = zh * ZLO + zl

    def at(y=y, x=x, z=None, zh=zh, zl=zl, c=c):
        if z is not None:
            zh, zl = lax.div(z, ZLO), lax.rem(z, ZLO)
        return {"src": y, "snk": zh * NX + x, "slab": zl * 2 + c}

    def turn(value, by, size):
        return lax.rem(value + by, size)

    def copy(source, target, send, recv, device):
        return pltpu.make_async_remote_copy(
            src_ref=source, dst_ref=target, send_sem=send, recv_sem=recv, device_id=device, device_id_type=MESH
        )

    fetches = [
        pltpu.make_async_copy(momenta, mom, in_s.at[0]),
        pltpu.make_async_copy(source_times, st, in_s.at[1]),
        pltpu.make_async_copy(eigvecs.at[1 - c], eig.at[1 - c], in_s.at[2]),
        pltpu.make_async_copy(eigvecs.at[c], eig.at[c], in_s.at[3]),
    ]
    loads = []
    for t in range(2):
        for s in range(2):
            loads.append(pltpu.make_async_copy(peram.at[t, s], pcat.at[t, s, :, pl.ds(0, NEV)], p_s.at[t, s]))
    for each in fetches:
        each.start()

    barrier = pltpu.get_barrier_semaphore()
    peers = [at(y=turn(y, d, NY)) for d in (2, 1, 3)] + [at(z=turn(z, k, NZ)) for k in (1, 7)]
    peers += [at(x=turn(x, d, NX)) for d in (1, 3)] + [at(c=1 - c)]
    for peer in peers:
        pl.semaphore_signal(barrier, inc=1, device_id=peer, device_id_type=MESH)

    def tell(round, height):
        for peer in [at(z=turn(z, k, NZ)) for k in (height, NZ - height)] + [at(x=turn(x, d, NX)) for d in (1, 3)]:
            pl.semaphore_signal(known.at[round], inc=1, device_id=peer, device_id_type=MESH)

    fetches[0].wait()
    fetches[2].wait()

    sends = []
    sibling = at(c=1 - c)

    row = lax.broadcasted_iota(jnp.int32, (8, SITES), 0)
    site = lax.broadcasted_iota(jnp.int32, (8, SITES), 1)

    def component(k):
        value = jnp.zeros((8, SITES), jnp.int32)
        for d in range(NY):
            value = jnp.where((row & 3) == d, mom[turn(y, d, NY), k], value)
        return value

    plane = y * NZ + slab
    fx = ((component(0) * (site & (LX - 1))) & (LX - 1)).astype(F32) / LX
    fy = ((component(1) * ((site >> 5) & (LY - 1))) & (LY - 1)).astype(F32) / LY
    fz = ((component(2) * plane) & (LZ - 1)).astype(F32) / LZ
    angle = 2.0 * math.pi * (fx + fy + fz - jnp.where(row < 4, 0.0, 0.25))
    trig[...] = jnp.cos(angle).T

    def prepare(t):
        vt[t] = eig[t].T
        for r in range(0, SITES, 256):
            vs[t, r : r + 256] = -jnp.dot(eig[t, r : r + 256], swap, preferred_element_type=F32).astype(BF16)

    def phase(t, d, slot):
        for r in range(0, SITES, 128):
            cosine = trig[r : r + 128, d : d + 1]
            sine = trig[r : r + 128, d + 4 : d + 5]
            phased = cosine * eig[t, r : r + 128].astype(F32) + sine * vs[t, r : r + 128].astype(F32)
            w[slot, r : r + 128] = phased.astype(BF16)

    swap = swap_matrix()
    prepare(1 - c)

    pair = {}
    along = {}
    turns = ((1, 2), (1, 1), (0, 2), (1, 3), (0, 1), (0, 3), (1, 0), (0, 0))

    def time(other):
        return 1 - c if other else c

    slots = [turn((b % 2) * ZLO + b // 2 + 2 * NZ - 2, -z, NZ) for b in range(NZ)]

    def ready(d):
        pair[d].wait_recv()
        for b in range(NZ):
            ysend[d - 1, slots[b]] = (mine[d, b] + d2d[d, b].astype(F32)).astype(BF16)

    def go_along(d, part):
        there = pl.ds(4 * part, 4)
        along[d, part] = copy(ysend.at[d - 1, there], yrecv.at[d - 1, there], y_s.at[d - 1, part],
                              y_r.at[d - 1, part], at(y=turn(y, d, NY)))
        along[d, part].start()

    after = {2: ((2, 0),), 1: ((1, 0), (2, 1)), 3: ((3, 0), (1, 1), (3, 1))}
    phase(1 - c, 2, 0)
    for k, (other, d) in enumerate(turns):
        if k == 1:
            fetches[3].wait()
            for each in loads:
                each.start()
            prepare(c)
        if k + 1 < len(turns):
            phase(time(turns[k + 1][0]), turns[k + 1][1], (k + 1) % 2)
        gram = jnp.dot(vt[time(other)], w[k % 2], preferred_element_type=F32)
        value = (gram[:NEV] + turned(gram[NEV:])).reshape(NZ, ROWS, COLS)
        if other:
            dsend[d] = value.astype(BF16)
            pair[d] = copy(dsend.at[d], d2d.at[d], d2d_s.at[d], d2d_r.at[d], sibling)
        else:
            mine[d] = value
        if k == 1:
            pl.semaphore_wait(barrier, len(peers))
            for each in (2, 1):
                pair[each].start()
            tell(0, 1)
        elif k and other:
            pair[d].start()
        elif k and d:
            ready(d)
            for each in after[d]:
                go_along(*each)
        if k == 6:
            pl.semaphore_wait(known.at[0], 4)
            tell(1, 2)
    sends += list(pair.values()) + list(along.values())

    for each in loads:
        each.wait()
    for t in range(2):
        for s in range(2):
            for k in range(4):
                pcat[t, s, k, NEV:] = jnp.dot(pcat[t, s, k, :NEV], swap, preferred_element_type=F32).astype(BF16)

    pair[0].wait_recv()
    pl.semaphore_wait(known.at[1], 4)

    def summed(r):
        block = block_of(turn(z, r, NZ))
        total = mine[0, block] + d2d[0, block].astype(F32)
        for d in range(3):
            total += yrecv[d, (r + 6) % NZ].astype(F32)
        return total.astype(BF16)

    for part, heights in ((0, (4, 3, 5, 2)), (1, (6, 1, 7))):
        for d in (2, 1, 3):
            along[d, part].wait_recv()
        for dz in heights:
            q[dz] = summed(dz)
            each = copy(q.at[dz], zrecv.at[z], z_s.at[dz], z_r.at[z], at(z=turn(z, dz, NZ)))
            each.start()
            sends.append(each)
    zrecv[z] = summed(0)
    for dz in range(1, NZ):
        come = turn(z, dz, NZ)
        copy(q.at[dz], zrecv.at[come], z_s.at[dz], z_r.at[come], at(z=come)).wait_recv()
    for g in range(2):
        total = zrecv[g * ZLO].astype(F32)
        for k in range(1, ZLO):
            total += zrecv[g * ZLO + k].astype(F32)
        es[y, g] = total.astype(BF16)

    for d in (2, 1, 3):
        each = copy(es.at[y], es.at[y], es_s.at[d - 1], es_r.at[y], at(y=turn(y, d, NY)))
        each.start()
        sends.append(each)
    fetches[1].wait()
    for s in range(2):
        wanted[s] = jnp.full((8, COLS), st[s], jnp.int32)
    for d in (1, 3, 2):
        m = turn(y, d, NY)
        copy(es.at[m], es.at[m], es_s.at[d - 1], es_r.at[m], at(y=m)).wait_recv()

    def picked(m, s):
        total = jnp.zeros((ROWS, COLS), F32)
        for g in range(2):
            total += jnp.where(wanted[s][0:1] == 2 * (g * NX + x) + c, es[m, g].astype(F32), 0.0)
        return total.astype(BF16)

    for d, k in ((2, 0), (2, 1), (1, 0), (1, 1), (3, 0), (3, 1), (0, 1)):
        m, s = turn(x, d, NX), turn(c, k, 2)
        sel[d, k] = picked(m, s)
        each = copy(sel.at[d, k], srecv.at[x, c], sel_s.at[d, k], sel_r.at[x, c], at(x=m, c=s))
        each.start()
        sends.append(each)

    opposite = copy(es.at[:, 1 - zh], ep, ep_s, ep_r, at(z=turn(z, ZLO, NZ)))
    opposite.start()
    sends.append(opposite)

    srecv[x, c] = picked(x, c)
    for d, k in ((0, 1), (1, 0), (1, 1), (3, 0), (3, 1), (2, 0), (2, 1)):
        come, core = turn(x, d, NX), turn(c, k, 2)
        copy(sel.at[d, k], srecv.at[come, core], sel_s.at[d, k], sel_r.at[come, core], at(x=come, c=core) if d else sibling).wait_recv()
    total = jnp.zeros((ROWS, COLS), F32)
    for k in range(NX):
        for core in range(2):
            total += srecv[k, core].astype(F32)
    src[c, x, 0] = total.astype(BF16)

    groups = ((0, 1), (1, 2), (6, 2), (3, 3))

    def piece(s, m, group):
        return src.at[s, m, pl.ds(groups[group][0], groups[group][1])]

    for dz in (1, 7, 2, 6, 3, 5, 4):
        each = copy(src.at[c, x, 0], src.at[c, x, NZ - dz], up_s.at[dz], up_r.at[NZ - dz], at(z=turn(z, dz, NZ)))
        each.start()
        sends.append(each)

    def share(group, d):
        m = turn(x, NX - d, NX)
        each = copy(piece(c, m, group), piece(c, m, group), sib_s.at[d, group], sib_r.at[d, group], sibling)
        each.start()
        sends.append(each)

    def spread(group):
        for d in (2, 1, 3):
            each = copy(piece(c, x, group), piece(c, x, group), out_s.at[d - 1, group], out_r.at[d - 1, group],
                        at(x=turn(x, d, NX)))
            each.start()
            sends.append(each)
        share(group, 0)

    spread(0)

    def come_up(group):
        for k in range(groups[group][0], sum(groups[group])):
            copy(src.at[c, x, 0], src.at[c, x, k], up_s.at[1], up_r.at[k], at(z=turn(z, k, NZ))).wait_recv()
        spread(group)

    def come_out(group, d):
        m = turn(x, NX - d, NX)
        copy(piece(c, m, group), piece(c, m, group), out_s.at[d - 1, group], out_r.at[d - 1, group], at(x=m)).wait_recv()

    def come_shared(group, d):
        m = turn(x, NX - d, NX)
        copy(piece(1 - c, m, group), piece(1 - c, m, group), sib_s.at[d, group], sib_r.at[d, group], sibling).wait_recv()

    opposite.wait_recv()
    near = copy(ep, sink.at[c], sink_s, sink_r.at[c], sibling)
    far = copy(es.at[:, zh], sink.at[c], sink_s, sink_r.at[c], sibling)

    @pl.when(c == zh)
    def _():
        near.start()
        for m in range(NY):
            sink[c, m] = es[m, zh]

    @pl.when(c != zh)
    def _():
        far.start()
        sink[c] = ep[...]

    sends.append(near)
    come_up(1)
    come_up(2)

    copy(ep, sink.at[1 - c], sink_s, sink_r.at[1 - c], sibling).wait_recv()
    for t in range(2):
        left = sink[t].astype(F32).reshape(NY * ROWS, COLS).astype(BF16)
        for s in range(2):
            for k in range(4):
                value = jnp.dot(left, pcat[t, s, k], preferred_element_type=F32)
                value = value.reshape(NY, ROWS, COLS).astype(BF16)
                for m in range(NY):
                    half[s, m, 4 * t + k] = value[m]

    come_up(3)
    for group in (0, 1, 2):
        for d in (1, 3, 2):
            come_out(group, d)
            share(group, d)


    def flat(value):
        return value.astype(F32).reshape(NEV, COLS).astype(BF16)

    def finish(s, d):
        slot, m = d % 2, turn(x, NX - d, NX)
        heights = [(b % 2) * ZLO + b // 2 for b in range(NZ)]
        rows = [src[s, m, turn(height + NZ, -z, NZ)].astype(F32) for height in heights]
        rows = jnp.concatenate(rows, axis=0).astype(BF16)
        both[slot, :NEV] = rows
        both[slot, NEV:] = jnp.dot(rows, swap, preferred_element_type=F32).astype(BF16)
        value = lax.dot_general(flat(half[s, m]), both[slot], (((1,), (1,)), ((), ())), preferred_element_type=F32)
        value = value.reshape(2, 4, ROWS, COLS)
        for t in range(2):
            blocks[m, t, s] = value[t]

    finish(c, 0)
    for group in range(4):
        come_shared(group, 0)
    finish(1 - c, 0)
    for d in (1, 3, 2):
        come_out(3, d)
        share(3, d)
    for d in (1, 3, 2):
        finish(c, d)
    for d in (1, 3, 2):
        for group in range(4):
            come_shared(group, d)
        finish(1 - c, d)

    for each in sends:
        each.wait_send()


def exchanged(eigvecs, momenta, source_times, perambulator):
    dma = pltpu.SemaphoreType.DMA

    def vmem(*lead, kind=BF16):
        return pltpu.VMEM(lead + (ROWS, COLS), kind)

    return pl.pallas_call(
        exchange,
        out_shape=jax.ShapeDtypeStruct((NY, 2, 2, 4, ROWS, COLS), F32),
        in_specs=[pl.BlockSpec(memory_space=pltpu.HBM)] * 4,
        out_specs=pl.BlockSpec(memory_space=pltpu.VMEM),
        scratch_shapes=[
            vmem(2, 4, 8), vmem(2, 4, 8), pltpu.VMEM((2, COLS, COLS), BF16),
            pltpu.VMEM((2, SITES, COLS), BF16), pltpu.SMEM((NY, 3), jnp.int32), pltpu.SMEM((2,), jnp.int32),
            pltpu.VMEM((SITES, 8), F32), pltpu.VMEM((2, COLS, SITES), BF16), pltpu.VMEM((2, SITES, COLS), BF16),
            pltpu.VMEM((2, SITES, COLS), BF16),
            vmem(4, 8), vmem(4, 8), vmem(4, 8, kind=F32), vmem(3, 8), vmem(3, 8), vmem(8), vmem(8),
            pltpu.VMEM((2, 8, COLS), jnp.int32), vmem(4, 2), vmem(4, 2), vmem(4, 2), vmem(4), vmem(2, 4),
            pltpu.VMEM((2, 2, 4, COLS, COLS), BF16),
            dma((4,)), dma((2, 2)), dma((4,)), dma((4,)), dma((3, 2)), dma((3, 2)), dma((8,)), dma((8,)),
            dma((4, 2)), dma((4, 2)),
            dma((3,)), dma((4,)), dma, dma, dma, dma((2,)), dma((8,)), dma((8,)),
            dma((3, 4)), dma((3, 4)), dma((4, 4)), dma((4, 4)), pltpu.SemaphoreType.REGULAR((2,)),
        ],
        compiler_params=pltpu.CompilerParams(
            collective_id=0, has_side_effects=True, vmem_limit_bytes=50 * 1024 * 1024
        ),
    )(eigvecs, momenta, source_times, perambulator)


def local(eigvecs, perambulator, momenta, source_times):
    def here(value):
        return pltpu.with_memory_space_constraint(value, pltpu.HBM)

    return exchanged(here(eigvecs), here(momenta), here(source_times), here(perambulator))


def solution(mesh):
    placed = (P("snk", ("src", "slab"), None), P("snk", "src", None, None, None), P(), P("src"))
    return jax.shard_map(
        local,
        mesh=mesh,
        in_specs=placed,
        out_specs=P(None, "snk", "src", None, "slab", None),
        check_vma=False,
    )
```

```python
import math

import jax
import jax.numpy as jnp
from jax import lax
from jax.experimental import pallas as pl
from jax.experimental.pallas import tpu as pltpu
from jax.sharding import PartitionSpec as P

LX = 32
LY = 32
LZ = 32
NX = 4
NY = 4
NZ = 8
ZLO = 4
NEV = 192
COLS = 2 * NEV
SITES = LX * LY
ROWS = 24
MESH = pl.DeviceIdType.MESH
F32 = jnp.float32
BF16 = jnp.bfloat16


def block_of(z):
    return lax.rem(z, ZLO) * 2 + lax.div(z, ZLO)


def turned(columns):
    lane = lax.broadcasted_iota(jnp.int32, columns.shape, 1)
    return pltpu.roll(columns, NEV, 1) * jnp.where(lane < NEV, 1.0, -1.0)


def swap_matrix():
    at_row = lax.broadcasted_iota(jnp.int32, (COLS, COLS), 0)
    at_col = lax.broadcasted_iota(jnp.int32, (COLS, COLS), 1)
    return (jnp.where(at_col == at_row + NEV, 1.0, 0.0) - jnp.where(at_row == at_col + NEV, 1.0, 0.0)).astype(BF16)


def exchange(eigvecs, momenta, source_times, peram, blocks, src, half, both, eig, mom, st, trig, vt, vs, w, dsend, d2d,
             mine, ysend, yrecv, q, zrecv, wanted, sel, srecv, es, ep, sink, pcat, zearly, far, come,
             in_s, p_s, d2d_s, d2d_r, y_s, y_r, z_s, z_r, sel_s, sel_r,
             es_s, es_r, ep_s, ep_r, sink_s, sink_r, up_s, up_r, out_s, out_r, sib_s, sib_r, ze_s, ze_r, far_s, far_r):
    y = lax.axis_index("src")
    snk = lax.axis_index("snk")
    slab = lax.axis_index("slab")
    zh, x = lax.div(snk, NX), lax.rem(snk, NX)
    zl, c = lax.div(slab, 2), lax.rem(slab, 2)
    z = zh * ZLO + zl

    def at(y=y, x=x, z=None, zh=zh, zl=zl, c=c):
        if z is not None:
            zh, zl = lax.div(z, ZLO), lax.rem(z, ZLO)
        return {"src": y, "snk": zh * NX + x, "slab": zl * 2 + c}

    def turn(value, by, size):
        return lax.rem(value + by, size)

    def copy(source, target, send, recv, device):
        return pltpu.make_async_remote_copy(
            src_ref=source, dst_ref=target, send_sem=send, recv_sem=recv, device_id=device, device_id_type=MESH
        )

    fetches = [
        pltpu.make_async_copy(momenta, mom, in_s.at[0]),
        pltpu.make_async_copy(source_times, st, in_s.at[1]),
        pltpu.make_async_copy(eigvecs.at[1 - c], eig.at[1 - c], in_s.at[2]),
        pltpu.make_async_copy(eigvecs.at[c], eig.at[c], in_s.at[3]),
    ]
    loads = []
    for t in range(2):
        for s in range(2):
            loads.append(pltpu.make_async_copy(peram.at[t, s], pcat.at[t, s, :, pl.ds(0, NEV)], p_s.at[t, s]))
    for each in fetches:
        each.start()

    barrier = pltpu.get_barrier_semaphore()
    peers = [at(z=turn(z, k, NZ)) for k in (4, 3, 5)] + [at(x=turn(x, 2, NX), c=k) for k in range(2)]
    peers += [at(y=turn(y, 2, NY))] + [at(z=turn(z, k, NZ)) for k in (2, 6)]
    peers += [at(x=turn(x, d, NX), c=k) for d in (1, 3) for k in range(2)]
    peers += [at(y=turn(y, d, NY)) for d in (1, 3)] + [at(z=turn(z, k, NZ)) for k in (1, 7)] + [at(c=1 - c)]
    for peer in peers:
        pl.semaphore_signal(barrier, inc=1, device_id=peer, device_id_type=MESH)
    fetches[0].wait()
    fetches[2].wait()

    sends = []
    sibling = at(c=1 - c)

    row = lax.broadcasted_iota(jnp.int32, (8, SITES), 0)
    site = lax.broadcasted_iota(jnp.int32, (8, SITES), 1)

    def component(k):
        value = jnp.zeros((8, SITES), jnp.int32)
        for d in range(NY):
            value = jnp.where((row & 3) == d, mom[turn(y, d, NY), k], value)
        return value

    plane = y * NZ + slab
    fx = ((component(0) * (site & (LX - 1))) & (LX - 1)).astype(F32) / LX
    fy = ((component(1) * ((site >> 5) & (LY - 1))) & (LY - 1)).astype(F32) / LY
    fz = ((component(2) * plane) & (LZ - 1)).astype(F32) / LZ
    angle = 2.0 * math.pi * (fx + fy + fz - jnp.where(row < 4, 0.0, 0.25))
    trig[...] = jnp.cos(angle).T

    def prepare(t):
        vt[t] = eig[t].T
        for r in range(0, SITES, 256):
            vs[t, r : r + 256] = -jnp.dot(eig[t, r : r + 256], swap, preferred_element_type=F32).astype(BF16)

    def phase(t, d, slot):
        for r in range(0, SITES, 128):
            cosine = trig[r : r + 128, d : d + 1]
            sine = trig[r : r + 128, d + 4 : d + 5]
            phased = cosine * eig[t, r : r + 128].astype(F32) + sine * vs[t, r : r + 128].astype(F32)
            w[slot, r : r + 128] = phased.astype(BF16)

    swap = swap_matrix()
    prepare(1 - c)

    pair = {}
    along = {}
    turns = ((1, 2), (1, 1), (0, 2), (1, 3), (0, 1), (0, 3), (1, 0), (0, 0))

    def time(other):
        return 1 - c if other else c

    slots = [turn((b % 2) * ZLO + b // 2 + 2 * NZ - 2, -z, NZ) for b in range(NZ)]

    def ready(d):
        pair[d].wait_recv()
        for b in range(NZ):
            ysend[d - 1, slots[b]] = (mine[d, b] + d2d[d, b].astype(F32)).astype(BF16)

    def go_along(d, part):
        there = pl.ds(4 * part, 4)
        along[d, part] = copy(ysend.at[d - 1, there], yrecv.at[d - 1, there], y_s.at[d - 1, part],
                              y_r.at[d - 1, part], at(y=turn(y, d, NY)))
        along[d, part].start()

    def early(dz):
        return copy(ysend.at[1, (dz + 6) % NZ], zearly.at[z], ze_s.at[dz], ze_r.at[z], at(z=turn(z, dz, NZ)))

    phase(1 - c, 2, 0)
    for k, (other, d) in enumerate(turns):
        if k == 1:
            fetches[3].wait()
            for each in loads:
                each.start()
            prepare(c)
        if k + 1 < len(turns):
            phase(time(turns[k + 1][0]), turns[k + 1][1], (k + 1) % 2)
        gram = jnp.dot(vt[time(other)], w[k % 2], preferred_element_type=F32)
        value = (gram[:NEV] + turned(gram[NEV:])).reshape(NZ, ROWS, COLS)
        if other:
            dsend[d] = value.astype(BF16)
            pair[d] = copy(dsend.at[d], d2d.at[d], d2d_s.at[d], d2d_r.at[d], sibling)
        else:
            mine[d] = value
        if k == 1:
            pl.semaphore_wait(barrier, len(peers))
            for each in (2, 1):
                pair[each].start()
        elif k and other:
            pair[d].start()
        elif k and d:
            ready(d)
            if d == 2:
                for dz in (4, 3, 5, 2, 6, 1, 7):
                    early(dz).start()
                zearly[z] = ysend[1, 6]
            else:
                go_along(d, 0)
                go_along(d, 1)
    sends += list(pair.values()) + list(along.values())

    for each in loads:
        each.wait()
    for t in range(2):
        for s in range(2):
            for k in range(4):
                pcat[t, s, k, NEV:] = jnp.dot(pcat[t, s, k, :NEV], swap, preferred_element_type=F32).astype(BF16)

    pair[0].wait_recv()

    def summed(r):
        block = block_of(turn(z, r, NZ))
        total = mine[0, block] + d2d[0, block].astype(F32)
        for d in (1, 3):
            total += yrecv[d - 1, (r + 6) % NZ].astype(F32)
        return total.astype(BF16)

    to_far = copy(far, come, far_s, far_r, at(y=turn(y, 2, NY)))
    sends += [early(dz) for dz in range(1, NZ)] + [to_far]

    for part, heights in ((0, (4, 3, 5, 2)), (1, (6, 1, 7))):
        for d in (1, 3):
            along[d, part].wait_recv()
        for dz in heights:
            q[dz] = summed(dz)
            each = copy(q.at[dz], zrecv.at[z], z_s.at[dz], z_r.at[z], at(z=turn(z, dz, NZ)))
            each.start()
            sends.append(each)
        if part == 0:
            for dz in range(1, NZ):
                height = turn(z, dz, NZ)
                copy(q.at[dz], zearly.at[height], ze_s.at[dz], ze_r.at[height], at(z=height)).wait_recv()
            for g in range(2):
                total = zearly[g * ZLO].astype(F32)
                for k in range(1, ZLO):
                    total += zearly[g * ZLO + k].astype(F32)
                far[g] = total.astype(BF16)
            to_far.start()
    zrecv[z] = summed(0)
    for dz in range(1, NZ):
        height = turn(z, dz, NZ)
        copy(q.at[dz], zrecv.at[height], z_s.at[dz], z_r.at[height], at(z=height)).wait_recv()
    to_far.wait_recv()
    for g in range(2):
        total = zrecv[g * ZLO].astype(F32) + come[g].astype(F32)
        for k in range(1, ZLO):
            total += zrecv[g * ZLO + k].astype(F32)
        es[y, g] = total.astype(BF16)

    for d in (2, 1, 3):
        each = copy(es.at[y], es.at[y], es_s.at[d - 1], es_r.at[y], at(y=turn(y, d, NY)))
        each.start()
        sends.append(each)
    fetches[1].wait()
    for s in range(2):
        wanted[s] = jnp.full((8, COLS), st[s], jnp.int32)
    for d in (1, 3, 2):
        m = turn(y, d, NY)
        copy(es.at[m], es.at[m], es_s.at[d - 1], es_r.at[m], at(y=m)).wait_recv()

    def picked(m, s):
        total = jnp.zeros((ROWS, COLS), F32)
        for g in range(2):
            total += jnp.where(wanted[s][0:1] == 2 * (g * NX + x) + c, es[m, g].astype(F32), 0.0)
        return total.astype(BF16)

    for d, k in ((2, 0), (2, 1), (1, 0), (1, 1), (3, 0), (3, 1), (0, 1)):
        m, s = turn(x, d, NX), turn(c, k, 2)
        sel[d, k] = picked(m, s)
        each = copy(sel.at[d, k], srecv.at[x, c], sel_s.at[d, k], sel_r.at[x, c], at(x=m, c=s))
        each.start()
        sends.append(each)

    opposite = copy(es.at[:, 1 - zh], ep, ep_s, ep_r, at(z=turn(z, ZLO, NZ)))
    opposite.start()
    sends.append(opposite)

    srecv[x, c] = picked(x, c)
    for d, k in ((0, 1), (1, 0), (1, 1), (3, 0), (3, 1), (2, 0), (2, 1)):
        giver, core = turn(x, d, NX), turn(c, k, 2)
        copy(sel.at[d, k], srecv.at[giver, core], sel_s.at[d, k], sel_r.at[giver, core],
             at(x=giver, c=core) if d else sibling).wait_recv()
    total = jnp.zeros((ROWS, COLS), F32)
    for k in range(NX):
        for core in range(2):
            total += srecv[k, core].astype(F32)
    src[c, x, 0] = total.astype(BF16)

    groups = ((0, 1), (1, 2), (6, 2), (3, 3))

    def piece(s, m, group):
        return src.at[s, m, pl.ds(groups[group][0], groups[group][1])]

    for dz in (1, 7, 2, 6, 3, 5, 4):
        each = copy(src.at[c, x, 0], src.at[c, x, NZ - dz], up_s.at[dz], up_r.at[NZ - dz], at(z=turn(z, dz, NZ)))
        each.start()
        sends.append(each)

    def share(group, d):
        m = turn(x, NX - d, NX)
        each = copy(piece(c, m, group), piece(c, m, group), sib_s.at[d, group], sib_r.at[d, group], sibling)
        each.start()
        sends.append(each)

    def spread(group):
        for d in (2, 1, 3):
            each = copy(piece(c, x, group), piece(c, x, group), out_s.at[d - 1, group], out_r.at[d - 1, group],
                        at(x=turn(x, d, NX)))
            each.start()
            sends.append(each)
        share(group, 0)

    spread(0)

    def come_up(group):
        for k in range(groups[group][0], sum(groups[group])):
            copy(src.at[c, x, 0], src.at[c, x, k], up_s.at[1], up_r.at[k], at(z=turn(z, k, NZ))).wait_recv()
        spread(group)

    def come_out(group, d):
        m = turn(x, NX - d, NX)
        copy(piece(c, m, group), piece(c, m, group), out_s.at[d - 1, group], out_r.at[d - 1, group], at(x=m)).wait_recv()

    def come_shared(group, d):
        m = turn(x, NX - d, NX)
        copy(piece(1 - c, m, group), piece(1 - c, m, group), sib_s.at[d, group], sib_r.at[d, group], sibling).wait_recv()

    opposite.wait_recv()
    near = copy(ep, sink.at[c], sink_s, sink_r.at[c], sibling)
    far = copy(es.at[:, zh], sink.at[c], sink_s, sink_r.at[c], sibling)

    @pl.when(c == zh)
    def _():
        near.start()
        for m in range(NY):
            sink[c, m] = es[m, zh]

    @pl.when(c != zh)
    def _():
        far.start()
        sink[c] = ep[...]

    sends.append(near)
    come_up(1)
    come_up(2)

    copy(ep, sink.at[1 - c], sink_s, sink_r.at[1 - c], sibling).wait_recv()
    for t in range(2):
        left = sink[t].astype(F32).reshape(NY * ROWS, COLS).astype(BF16)
        for s in range(2):
            for k in range(4):
                value = jnp.dot(left, pcat[t, s, k], preferred_element_type=F32)
                value = value.reshape(NY, ROWS, COLS).astype(BF16)
                for m in range(NY):
                    half[s, m, 4 * t + k] = value[m]

    come_up(3)
    for group in (0, 1, 2):
        for d in (1, 3, 2):
            come_out(group, d)
            share(group, d)


    def flat(value):
        return value.astype(F32).reshape(NEV, COLS).astype(BF16)

    def finish(s, d):
        slot, m = d % 2, turn(x, NX - d, NX)
        heights = [(b % 2) * ZLO + b // 2 for b in range(NZ)]
        rows = [src[s, m, turn(height + NZ, -z, NZ)].astype(F32) for height in heights]
        rows = jnp.concatenate(rows, axis=0).astype(BF16)
        both[slot, :NEV] = rows
        both[slot, NEV:] = jnp.dot(rows, swap, preferred_element_type=F32).astype(BF16)
        value = lax.dot_general(flat(half[s, m]), both[slot], (((1,), (1,)), ((), ())), preferred_element_type=F32)
        value = value.reshape(2, 4, ROWS, COLS)
        for t in range(2):
            blocks[m, t, s] = value[t]

    finish(c, 0)
    for group in range(4):
        come_shared(group, 0)
    finish(1 - c, 0)
    for d in (1, 3, 2):
        come_out(3, d)
        share(3, d)
    for d in (1, 3, 2):
        finish(c, d)
    for d in (1, 3, 2):
        for group in range(4):
            come_shared(group, d)
        finish(1 - c, d)

    for each in sends:
        each.wait_send()


def exchanged(eigvecs, momenta, source_times, perambulator):
    dma = pltpu.SemaphoreType.DMA

    def vmem(*lead, kind=BF16):
        return pltpu.VMEM(lead + (ROWS, COLS), kind)

    return pl.pallas_call(
        exchange,
        out_shape=jax.ShapeDtypeStruct((NY, 2, 2, 4, ROWS, COLS), F32),
        in_specs=[pl.BlockSpec(memory_space=pltpu.HBM)] * 4,
        out_specs=pl.BlockSpec(memory_space=pltpu.VMEM),
        scratch_shapes=[
            vmem(2, 4, 8), vmem(2, 4, 8), pltpu.VMEM((2, COLS, COLS), BF16),
            pltpu.VMEM((2, SITES, COLS), BF16), pltpu.SMEM((NY, 3), jnp.int32), pltpu.SMEM((2,), jnp.int32),
            pltpu.VMEM((SITES, 8), F32), pltpu.VMEM((2, COLS, SITES), BF16), pltpu.VMEM((2, SITES, COLS), BF16),
            pltpu.VMEM((2, SITES, COLS), BF16),
            vmem(4, 8), vmem(4, 8), vmem(4, 8, kind=F32), vmem(3, 8), vmem(3, 8), vmem(8), vmem(8),
            pltpu.VMEM((2, 8, COLS), jnp.int32), vmem(4, 2), vmem(4, 2), vmem(4, 2), vmem(4), vmem(2, 4),
            pltpu.VMEM((2, 2, 4, COLS, COLS), BF16), vmem(8), vmem(2), vmem(2),
            dma((4,)), dma((2, 2)), dma((4,)), dma((4,)), dma((3, 2)), dma((3, 2)), dma((8,)), dma((8,)),
            dma((4, 2)), dma((4, 2)),
            dma((3,)), dma((4,)), dma, dma, dma, dma((2,)), dma((8,)), dma((8,)),
            dma((3, 4)), dma((3, 4)), dma((4, 4)), dma((4, 4)), dma((8,)), dma((8,)), dma, dma,
        ],
        compiler_params=pltpu.CompilerParams(
            collective_id=0, has_side_effects=True, vmem_limit_bytes=50 * 1024 * 1024
        ),
    )(eigvecs, momenta, source_times, perambulator)


def local(eigvecs, perambulator, momenta, source_times):
    def here(value):
        return pltpu.with_memory_space_constraint(value, pltpu.HBM)

    return exchanged(here(eigvecs), here(momenta), here(source_times), here(perambulator))


def solution(mesh):
    placed = (P("snk", ("src", "slab"), None), P("snk", "src", None, None, None), P(), P("src"))
    return jax.shard_map(
        local,
        mesh=mesh,
        in_specs=placed,
        out_specs=P(None, "snk", "src", None, "slab", None),
        check_vma=False,
    )
```

```python
import math

import jax
import jax.numpy as jnp
from jax import lax
from jax.experimental import pallas as pl
from jax.experimental.pallas import tpu as pltpu
from jax.sharding import PartitionSpec as P

LX = 32
LY = 32
LZ = 32
NX = 4
NY = 4
NZ = 8
ZLO = 4
NEV = 192
COLS = 2 * NEV
SITES = LX * LY
ROWS = 24
MESH = pl.DeviceIdType.MESH
F32 = jnp.float32
BF16 = jnp.bfloat16


def block_of(z):
    return lax.rem(z, ZLO) * 2 + lax.div(z, ZLO)


def turned(columns):
    lane = lax.broadcasted_iota(jnp.int32, columns.shape, 1)
    return pltpu.roll(columns, NEV, 1) * jnp.where(lane < NEV, 1.0, -1.0)


def swap_matrix():
    at_row = lax.broadcasted_iota(jnp.int32, (COLS, COLS), 0)
    at_col = lax.broadcasted_iota(jnp.int32, (COLS, COLS), 1)
    return (jnp.where(at_col == at_row + NEV, 1.0, 0.0) - jnp.where(at_row == at_col + NEV, 1.0, 0.0)).astype(BF16)


def exchange(eigvecs, momenta, source_times, peram, blocks, src, half, both, eig, mom, st, trig, vt, vs, w, dsend, d2d,
             mine, ysend, yrecv, q, zrecv, wanted, sel, srecv, es, ep, sink, pcat, zearly, far, come,
             in_s, p_s, d2d_s, d2d_r, y_s, y_r, z_s, z_r, sel_s, sel_r,
             es_s, es_r, ep_s, ep_r, sink_s, sink_r, up_s, up_r, out_s, out_r, sib_s, sib_r, ze_s, ze_r, far_s, far_r):
    y = lax.axis_index("src")
    snk = lax.axis_index("snk")
    slab = lax.axis_index("slab")
    zh, x = lax.div(snk, NX), lax.rem(snk, NX)
    zl, c = lax.div(slab, 2), lax.rem(slab, 2)
    z = zh * ZLO + zl

    def at(y=y, x=x, z=None, zh=zh, zl=zl, c=c):
        if z is not None:
            zh, zl = lax.div(z, ZLO), lax.rem(z, ZLO)
        return {"src": y, "snk": zh * NX + x, "slab": zl * 2 + c}

    def turn(value, by, size):
        return lax.rem(value + by, size)

    def copy(source, target, send, recv, device):
        return pltpu.make_async_remote_copy(
            src_ref=source, dst_ref=target, send_sem=send, recv_sem=recv, device_id=device, device_id_type=MESH
        )

    fetches = [
        pltpu.make_async_copy(momenta, mom, in_s.at[0]),
        pltpu.make_async_copy(source_times, st, in_s.at[1]),
        pltpu.make_async_copy(eigvecs.at[1 - c], eig.at[1 - c], in_s.at[2]),
        pltpu.make_async_copy(eigvecs.at[c], eig.at[c], in_s.at[3]),
    ]
    loads = []
    for t in range(2):
        for s in range(2):
            loads.append(pltpu.make_async_copy(peram.at[t, s], pcat.at[t, s, :, pl.ds(0, NEV)], p_s.at[t, s]))
    for each in fetches:
        each.start()

    barrier = pltpu.get_barrier_semaphore()
    peers = [at(z=turn(z, k, NZ)) for k in (4, 3, 5)] + [at(x=turn(x, 2, NX), c=k) for k in range(2)]
    peers += [at(y=turn(y, 2, NY))] + [at(z=turn(z, k, NZ)) for k in (2, 6)]
    peers += [at(x=turn(x, d, NX), c=k) for d in (1, 3) for k in range(2)]
    peers += [at(y=turn(y, d, NY)) for d in (1, 3)] + [at(z=turn(z, k, NZ)) for k in (1, 7)] + [at(c=1 - c)]
    for peer in peers:
        pl.semaphore_signal(barrier, inc=1, device_id=peer, device_id_type=MESH)
    fetches[0].wait()
    fetches[2].wait()

    sends = []
    sibling = at(c=1 - c)

    row = lax.broadcasted_iota(jnp.int32, (8, SITES), 0)
    site = lax.broadcasted_iota(jnp.int32, (8, SITES), 1)

    def component(k):
        value = jnp.zeros((8, SITES), jnp.int32)
        for d in range(NY):
            value = jnp.where((row & 3) == d, mom[turn(y, d, NY), k], value)
        return value

    plane = y * NZ + slab
    fx = ((component(0) * (site & (LX - 1))) & (LX - 1)).astype(F32) / LX
    fy = ((component(1) * ((site >> 5) & (LY - 1))) & (LY - 1)).astype(F32) / LY
    fz = ((component(2) * plane) & (LZ - 1)).astype(F32) / LZ
    angle = 2.0 * math.pi * (fx + fy + fz - jnp.where(row < 4, 0.0, 0.25))
    trig[...] = jnp.cos(angle).T

    def prepare(t):
        vt[t] = eig[t].T
        for r in range(0, SITES, 256):
            vs[t, r : r + 256] = -jnp.dot(eig[t, r : r + 256], swap, preferred_element_type=F32).astype(BF16)

    def phase(t, d, slot):
        for r in range(0, SITES, 128):
            cosine = trig[r : r + 128, d : d + 1]
            sine = trig[r : r + 128, d + 4 : d + 5]
            phased = cosine * eig[t, r : r + 128].astype(F32) + sine * vs[t, r : r + 128].astype(F32)
            w[slot, r : r + 128] = phased.astype(BF16)

    swap = swap_matrix()
    prepare(1 - c)

    pair = {}
    along = {}
    turns = ((1, 2), (1, 1), (0, 2), (1, 3), (0, 1), (0, 3), (1, 0), (0, 0))

    def time(other):
        return 1 - c if other else c

    slots = [turn((b % 2) * ZLO + b // 2 + 2 * NZ - 2, -z, NZ) for b in range(NZ)]

    def ready(d):
        pair[d].wait_recv()
        for b in range(NZ):
            ysend[d - 1, slots[b]] = (mine[d, b] + d2d[d, b].astype(F32)).astype(BF16)

    def go_along(d, part):
        there = pl.ds(4 * part, 4)
        along[d, part] = copy(ysend.at[d - 1, there], yrecv.at[d - 1, there], y_s.at[d - 1, part],
                              y_r.at[d - 1, part], at(y=turn(y, d, NY)))
        along[d, part].start()

    def early(dz):
        return copy(ysend.at[1, (dz + 6) % NZ], zearly.at[z], ze_s.at[dz], ze_r.at[z], at(z=turn(z, dz, NZ)))

    phase(1 - c, 2, 0)
    for k, (other, d) in enumerate(turns):
        if k == 1:
            fetches[3].wait()
            for each in loads:
                each.start()
            prepare(c)
        if k + 1 < len(turns):
            phase(time(turns[k + 1][0]), turns[k + 1][1], (k + 1) % 2)
        gram = jnp.dot(vt[time(other)], w[k % 2], preferred_element_type=F32)
        value = (gram[:NEV] + turned(gram[NEV:])).reshape(NZ, ROWS, COLS)
        if other:
            dsend[d] = value.astype(BF16)
            pair[d] = copy(dsend.at[d], d2d.at[d], d2d_s.at[d], d2d_r.at[d], sibling)
        else:
            mine[d] = value
        if k == 1:
            pl.semaphore_wait(barrier, len(peers))
            for each in (2, 1):
                pair[each].start()
        elif k and other:
            pair[d].start()
        elif k and d:
            ready(d)
            if d == 2:
                for dz in (4, 3, 5, 2, 6, 1, 7):
                    early(dz).start()
                zearly[z] = ysend[1, 6]
            else:
                go_along(d, 0)
                go_along(d, 1)
    sends += list(pair.values()) + list(along.values())

    pair[0].wait_recv()

    def summed(r):
        block = block_of(turn(z, r, NZ))
        total = mine[0, block] + d2d[0, block].astype(F32)
        for d in (1, 3):
            total += yrecv[d - 1, (r + 6) % NZ].astype(F32)
        return total.astype(BF16)

    to_far = copy(far, come, far_s, far_r, at(y=turn(y, 2, NY)))
    sends += [early(dz) for dz in range(1, NZ)] + [to_far]

    for part, heights in ((0, (4, 3, 5, 2)), (1, (6, 1, 7))):
        for d in (1, 3):
            along[d, part].wait_recv()
        for dz in heights:
            q[dz] = summed(dz)
            each = copy(q.at[dz], zrecv.at[z], z_s.at[dz], z_r.at[z], at(z=turn(z, dz, NZ)))
            each.start()
            sends.append(each)
        if part == 0:
            for dz in range(1, NZ):
                height = turn(z, dz, NZ)
                copy(q.at[dz], zearly.at[height], ze_s.at[dz], ze_r.at[height], at(z=height)).wait_recv()
            for g in range(2):
                total = zearly[g * ZLO].astype(F32)
                for k in range(1, ZLO):
                    total += zearly[g * ZLO + k].astype(F32)
                far[g] = total.astype(BF16)
            to_far.start()
    zrecv[z] = summed(0)
    for dz in range(1, NZ):
        height = turn(z, dz, NZ)
        copy(q.at[dz], zrecv.at[height], z_s.at[dz], z_r.at[height], at(z=height)).wait_recv()
    to_far.wait_recv()
    for g in range(2):
        total = zrecv[g * ZLO].astype(F32) + come[g].astype(F32)
        for k in range(1, ZLO):
            total += zrecv[g * ZLO + k].astype(F32)
        es[y, g] = total.astype(BF16)

    for d in (2, 1, 3):
        each = copy(es.at[y], es.at[y], es_s.at[d - 1], es_r.at[y], at(y=turn(y, d, NY)))
        each.start()
        sends.append(each)
    for each in loads:
        each.wait()
    for t in range(2):
        for s in range(2):
            for k in range(4):
                pcat[t, s, k, NEV:] = jnp.dot(pcat[t, s, k, :NEV], swap, preferred_element_type=F32).astype(BF16)

    fetches[1].wait()
    for s in range(2):
        wanted[s] = jnp.full((8, COLS), st[s], jnp.int32)
    for d in (1, 3, 2):
        m = turn(y, d, NY)
        copy(es.at[m], es.at[m], es_s.at[d - 1], es_r.at[m], at(y=m)).wait_recv()

    def picked(m, s):
        total = jnp.zeros((ROWS, COLS), F32)
        for g in range(2):
            total += jnp.where(wanted[s][0:1] == 2 * (g * NX + x) + c, es[m, g].astype(F32), 0.0)
        return total.astype(BF16)

    for d, k in ((2, 0), (2, 1), (1, 0), (1, 1), (3, 0), (3, 1), (0, 1)):
        m, s = turn(x, d, NX), turn(c, k, 2)
        sel[d, k] = picked(m, s)
        each = copy(sel.at[d, k], srecv.at[x, c], sel_s.at[d, k], sel_r.at[x, c], at(x=m, c=s))
        each.start()
        sends.append(each)

    opposite = copy(es.at[:, 1 - zh], ep, ep_s, ep_r, at(z=turn(z, ZLO, NZ)))
    opposite.start()
    sends.append(opposite)

    srecv[x, c] = picked(x, c)
    for d, k in ((0, 1), (1, 0), (1, 1), (3, 0), (3, 1), (2, 0), (2, 1)):
        giver, core = turn(x, d, NX), turn(c, k, 2)
        copy(sel.at[d, k], srecv.at[giver, core], sel_s.at[d, k], sel_r.at[giver, core],
             at(x=giver, c=core) if d else sibling).wait_recv()
    total = jnp.zeros((ROWS, COLS), F32)
    for k in range(NX):
        for core in range(2):
            total += srecv[k, core].astype(F32)
    src[c, x, 0] = total.astype(BF16)

    groups = ((0, 1), (1, 2), (6, 2), (3, 3))

    def piece(s, m, group):
        return src.at[s, m, pl.ds(groups[group][0], groups[group][1])]

    for dz in (1, 7, 2, 6, 3, 5, 4):
        each = copy(src.at[c, x, 0], src.at[c, x, NZ - dz], up_s.at[dz], up_r.at[NZ - dz], at(z=turn(z, dz, NZ)))
        each.start()
        sends.append(each)

    def share(group, d):
        m = turn(x, NX - d, NX)
        each = copy(piece(c, m, group), piece(c, m, group), sib_s.at[d, group], sib_r.at[d, group], sibling)
        each.start()
        sends.append(each)

    def spread(group):
        for d in (2, 1, 3):
            each = copy(piece(c, x, group), piece(c, x, group), out_s.at[d - 1, group], out_r.at[d - 1, group],
                        at(x=turn(x, d, NX)))
            each.start()
            sends.append(each)
        share(group, 0)

    spread(0)

    def come_up(group):
        for k in range(groups[group][0], sum(groups[group])):
            copy(src.at[c, x, 0], src.at[c, x, k], up_s.at[1], up_r.at[k], at(z=turn(z, k, NZ))).wait_recv()
        spread(group)

    def come_out(group, d):
        m = turn(x, NX - d, NX)
        copy(piece(c, m, group), piece(c, m, group), out_s.at[d - 1, group], out_r.at[d - 1, group], at(x=m)).wait_recv()

    def come_shared(group, d):
        m = turn(x, NX - d, NX)
        copy(piece(1 - c, m, group), piece(1 - c, m, group), sib_s.at[d, group], sib_r.at[d, group], sibling).wait_recv()

    opposite.wait_recv()
    near = copy(ep, sink.at[c], sink_s, sink_r.at[c], sibling)
    far = copy(es.at[:, zh], sink.at[c], sink_s, sink_r.at[c], sibling)

    @pl.when(c == zh)
    def _():
        near.start()
        for m in range(NY):
            sink[c, m] = es[m, zh]

    @pl.when(c != zh)
    def _():
        far.start()
        sink[c] = ep[...]

    sends.append(near)
    come_up(1)
    come_up(2)

    copy(ep, sink.at[1 - c], sink_s, sink_r.at[1 - c], sibling).wait_recv()
    for t in range(2):
        left = sink[t].astype(F32).reshape(NY * ROWS, COLS).astype(BF16)
        for s in range(2):
            for k in range(4):
                value = jnp.dot(left, pcat[t, s, k], preferred_element_type=F32)
                value = value.reshape(NY, ROWS, COLS).astype(BF16)
                for m in range(NY):
                    half[s, m, 4 * t + k] = value[m]

    come_up(3)
    for group in (0, 1, 2):
        for d in (1, 3, 2):
            come_out(group, d)
            share(group, d)


    def flat(value):
        return value.astype(F32).reshape(NEV, COLS).astype(BF16)

    def finish(s, d):
        slot, m = d % 2, turn(x, NX - d, NX)
        heights = [(b % 2) * ZLO + b // 2 for b in range(NZ)]
        rows = [src[s, m, turn(height + NZ, -z, NZ)].astype(F32) for height in heights]
        rows = jnp.concatenate(rows, axis=0).astype(BF16)
        both[slot, :NEV] = rows
        both[slot, NEV:] = jnp.dot(rows, swap, preferred_element_type=F32).astype(BF16)
        value = lax.dot_general(flat(half[s, m]), both[slot], (((1,), (1,)), ((), ())), preferred_element_type=F32)
        value = value.reshape(2, 4, ROWS, COLS)
        for t in range(2):
            blocks[m, t, s] = value[t]

    finish(c, 0)
    for group in range(4):
        come_shared(group, 0)
    finish(1 - c, 0)
    for d in (1, 3, 2):
        come_out(3, d)
        share(3, d)
    for d in (1, 3, 2):
        finish(c, d)
    for d in (1, 3, 2):
        for group in range(4):
            come_shared(group, d)
        finish(1 - c, d)

    for each in sends:
        each.wait_send()


def exchanged(eigvecs, momenta, source_times, perambulator):
    dma = pltpu.SemaphoreType.DMA

    def vmem(*lead, kind=BF16):
        return pltpu.VMEM(lead + (ROWS, COLS), kind)

    return pl.pallas_call(
        exchange,
        out_shape=jax.ShapeDtypeStruct((NY, 2, 2, 4, ROWS, COLS), F32),
        in_specs=[pl.BlockSpec(memory_space=pltpu.HBM)] * 4,
        out_specs=pl.BlockSpec(memory_space=pltpu.VMEM),
        scratch_shapes=[
            vmem(2, 4, 8), vmem(2, 4, 8), pltpu.VMEM((2, COLS, COLS), BF16),
            pltpu.VMEM((2, SITES, COLS), BF16), pltpu.SMEM((NY, 3), jnp.int32), pltpu.SMEM((2,), jnp.int32),
            pltpu.VMEM((SITES, 8), F32), pltpu.VMEM((2, COLS, SITES), BF16), pltpu.VMEM((2, SITES, COLS), BF16),
            pltpu.VMEM((2, SITES, COLS), BF16),
            vmem(4, 8), vmem(4, 8), vmem(4, 8, kind=F32), vmem(3, 8), vmem(3, 8), vmem(8), vmem(8),
            pltpu.VMEM((2, 8, COLS), jnp.int32), vmem(4, 2), vmem(4, 2), vmem(4, 2), vmem(4), vmem(2, 4),
            pltpu.VMEM((2, 2, 4, COLS, COLS), BF16), vmem(8), vmem(2), vmem(2),
            dma((4,)), dma((2, 2)), dma((4,)), dma((4,)), dma((3, 2)), dma((3, 2)), dma((8,)), dma((8,)),
            dma((4, 2)), dma((4, 2)),
            dma((3,)), dma((4,)), dma, dma, dma, dma((2,)), dma((8,)), dma((8,)),
            dma((3, 4)), dma((3, 4)), dma((4, 4)), dma((4, 4)), dma((8,)), dma((8,)), dma, dma,
        ],
        compiler_params=pltpu.CompilerParams(
            collective_id=0, has_side_effects=True, vmem_limit_bytes=50 * 1024 * 1024
        ),
    )(eigvecs, momenta, source_times, perambulator)


def local(eigvecs, perambulator, momenta, source_times):
    def here(value):
        return pltpu.with_memory_space_constraint(value, pltpu.HBM)

    return exchanged(here(eigvecs), here(momenta), here(source_times), here(perambulator))


def solution(mesh):
    placed = (P("snk", ("src", "slab"), None), P("snk", "src", None, None, None), P(), P("src"))
    return jax.shard_map(
        local,
        mesh=mesh,
        in_specs=placed,
        out_specs=P(None, "snk", "src", None, "slab", None),
        check_vma=False,
    )
```

```python
import math

import jax
import jax.numpy as jnp
from jax import lax
from jax.experimental import pallas as pl
from jax.experimental.pallas import tpu as pltpu
from jax.sharding import PartitionSpec as P

LX = 32
LY = 32
LZ = 32
NX = 4
NY = 4
NZ = 8
ZLO = 4
NEV = 192
COLS = 2 * NEV
SITES = LX * LY
ROWS = 24
MESH = pl.DeviceIdType.MESH
F32 = jnp.float32
BF16 = jnp.bfloat16


def block_of(z):
    return lax.rem(z, ZLO) * 2 + lax.div(z, ZLO)


def turned(columns):
    lane = lax.broadcasted_iota(jnp.int32, columns.shape, 1)
    return pltpu.roll(columns, NEV, 1) * jnp.where(lane < NEV, 1.0, -1.0)


def swap_matrix():
    at_row = lax.broadcasted_iota(jnp.int32, (COLS, COLS), 0)
    at_col = lax.broadcasted_iota(jnp.int32, (COLS, COLS), 1)
    return (jnp.where(at_col == at_row + NEV, 1.0, 0.0) - jnp.where(at_row == at_col + NEV, 1.0, 0.0)).astype(BF16)


def exchange(eigvecs, momenta, source_times, peram, blocks, src, half, both, eig, mom, st, trig, vt, vs, w, dsend, d2d,
             mine, ysend, yrecv, q, zrecv, wanted, sel, srecv, es, ep, sink, pcat, zearly, far, come,
             in_s, p_s, d2d_s, d2d_r, y_s, y_r, z_s, z_r, sel_s, sel_r,
             es_s, es_r, ep_s, ep_r, sink_s, sink_r, up_s, up_r, out_s, out_r, sib_s, sib_r, ze_s, ze_r, far_s, far_r):
    y = lax.axis_index("src")
    snk = lax.axis_index("snk")
    slab = lax.axis_index("slab")
    zh, x = lax.div(snk, NX), lax.rem(snk, NX)
    zl, c = lax.div(slab, 2), lax.rem(slab, 2)
    z = zh * ZLO + zl

    def at(y=y, x=x, z=None, zh=zh, zl=zl, c=c):
        if z is not None:
            zh, zl = lax.div(z, ZLO), lax.rem(z, ZLO)
        return {"src": y, "snk": zh * NX + x, "slab": zl * 2 + c}

    def turn(value, by, size):
        return lax.rem(value + by, size)

    def copy(source, target, send, recv, device):
        return pltpu.make_async_remote_copy(
            src_ref=source, dst_ref=target, send_sem=send, recv_sem=recv, device_id=device, device_id_type=MESH
        )

    fetches = [
        pltpu.make_async_copy(momenta, mom, in_s.at[0]),
        pltpu.make_async_copy(source_times, st, in_s.at[1]),
        pltpu.make_async_copy(eigvecs.at[1 - c], eig.at[1 - c], in_s.at[2]),
        pltpu.make_async_copy(eigvecs.at[c], eig.at[c], in_s.at[3]),
    ]
    loads = []
    for t in range(2):
        for s in range(2):
            loads.append(pltpu.make_async_copy(peram.at[t, s], pcat.at[t, s, :, pl.ds(0, NEV)], p_s.at[t, s]))
    for each in fetches:
        each.start()

    barrier = pltpu.get_barrier_semaphore()
    peers = [at(z=turn(z, k, NZ)) for k in (4, 3, 5)] + [at(x=turn(x, 2, NX), c=k) for k in range(2)]
    peers += [at(y=turn(y, 2, NY))] + [at(z=turn(z, k, NZ)) for k in (2, 6)]
    peers += [at(x=turn(x, d, NX), c=k) for d in (1, 3) for k in range(2)]
    peers += [at(y=turn(y, d, NY)) for d in (1, 3)] + [at(z=turn(z, k, NZ)) for k in (1, 7)] + [at(c=1 - c)]
    for peer in peers:
        pl.semaphore_signal(barrier, inc=1, device_id=peer, device_id_type=MESH)
    fetches[0].wait()
    fetches[2].wait()

    sends = []
    sibling = at(c=1 - c)

    row = lax.broadcasted_iota(jnp.int32, (8, SITES), 0)
    site = lax.broadcasted_iota(jnp.int32, (8, SITES), 1)

    def component(k):
        value = jnp.zeros((8, SITES), jnp.int32)
        for d in range(NY):
            value = jnp.where((row & 3) == d, mom[turn(y, d, NY), k], value)
        return value

    plane = y * NZ + slab
    fx = ((component(0) * (site & (LX - 1))) & (LX - 1)).astype(F32) / LX
    fy = ((component(1) * ((site >> 5) & (LY - 1))) & (LY - 1)).astype(F32) / LY
    fz = ((component(2) * plane) & (LZ - 1)).astype(F32) / LZ
    angle = 2.0 * math.pi * (fx + fy + fz - jnp.where(row < 4, 0.0, 0.25))
    trig[...] = jnp.cos(angle).T

    def prepare(t):
        vt[t] = eig[t].T
        for r in range(0, SITES, 256):
            vs[t, r : r + 256] = -jnp.dot(eig[t, r : r + 256], swap, preferred_element_type=F32).astype(BF16)

    def phase(t, d, slot):
        for r in range(0, SITES, 128):
            cosine = trig[r : r + 128, d : d + 1]
            sine = trig[r : r + 128, d + 4 : d + 5]
            phased = cosine * eig[t, r : r + 128].astype(F32) + sine * vs[t, r : r + 128].astype(F32)
            w[slot, r : r + 128] = phased.astype(BF16)

    swap = swap_matrix()
    prepare(1 - c)

    pair = {}
    along = {}
    turns = ((1, 2), (1, 1), (0, 2), (1, 3), (0, 1), (0, 3), (1, 0), (0, 0))

    def time(other):
        return 1 - c if other else c

    slots = [turn((b % 2) * ZLO + b // 2 + 2 * NZ - 2, -z, NZ) for b in range(NZ)]

    def ready(d):
        pair[d].wait_recv()
        for b in range(NZ):
            ysend[d - 1, slots[b]] = (mine[d, b] + d2d[d, b].astype(F32)).astype(BF16)

    def go_along(d, part):
        there = pl.ds(4 * part, 4)
        along[d, part] = copy(ysend.at[d - 1, there], yrecv.at[d - 1, there], y_s.at[d - 1, part],
                              y_r.at[d - 1, part], at(y=turn(y, d, NY)))
        along[d, part].start()

    def early(dz):
        return copy(ysend.at[1, (dz + 6) % NZ], zearly.at[z], ze_s.at[dz], ze_r.at[z], at(z=turn(z, dz, NZ)))

    phase(1 - c, 2, 0)
    for k, (other, d) in enumerate(turns):
        if k == 1:
            fetches[3].wait()
            for each in loads:
                each.start()
            prepare(c)
        if k + 1 < len(turns):
            phase(time(turns[k + 1][0]), turns[k + 1][1], (k + 1) % 2)
        gram = jnp.dot(vt[time(other)], w[k % 2], preferred_element_type=F32)
        value = (gram[:NEV] + turned(gram[NEV:])).reshape(NZ, ROWS, COLS)
        if other:
            dsend[d] = value.astype(BF16)
            pair[d] = copy(dsend.at[d], d2d.at[d], d2d_s.at[d], d2d_r.at[d], sibling)
        else:
            mine[d] = value
        if k == 1:
            pl.semaphore_wait(barrier, len(peers))
            for each in (2, 1):
                pair[each].start()
        elif k and other:
            pair[d].start()
        elif k and d:
            ready(d)
            if d == 2:
                for dz in (4, 3, 5, 2, 6, 1, 7):
                    early(dz).start()
                zearly[z] = ysend[1, 6]
            else:
                go_along(d, 0)
                go_along(d, 1)
    sends += list(pair.values()) + list(along.values())

    for each in loads:
        each.wait()
    for t in range(2):
        for s in range(2):
            for k in range(4):
                pcat[t, s, k, NEV:] = jnp.dot(pcat[t, s, k, :NEV], swap, preferred_element_type=F32).astype(BF16)

    pair[0].wait_recv()

    def summed(r):
        block = block_of(turn(z, r, NZ))
        total = mine[0, block] + d2d[0, block].astype(F32)
        for d in (1, 3):
            total += yrecv[d - 1, (r + 6) % NZ].astype(F32)
        return total.astype(BF16)

    to_far = copy(far, come, far_s, far_r, at(y=turn(y, 2, NY)))
    sends += [early(dz) for dz in range(1, NZ)] + [to_far]

    for part, heights in ((0, (4, 3, 5, 2)), (1, (6, 1, 7))):
        for d in (1, 3):
            along[d, part].wait_recv()
        for dz in heights:
            q[dz] = summed(dz)
            each = copy(q.at[dz], zrecv.at[z], z_s.at[dz], z_r.at[z], at(z=turn(z, dz, NZ)))
            each.start()
            sends.append(each)
        if part == 0:
            for dz in range(1, NZ):
                height = turn(z, dz, NZ)
                copy(q.at[dz], zearly.at[height], ze_s.at[dz], ze_r.at[height], at(z=height)).wait_recv()
            for g in range(2):
                total = zearly[g * ZLO].astype(F32)
                for k in range(1, ZLO):
                    total += zearly[g * ZLO + k].astype(F32)
                far[g] = total.astype(BF16)
            to_far.start()
    zrecv[z] = summed(0)
    for dz in range(1, NZ):
        height = turn(z, dz, NZ)
        copy(q.at[dz], zrecv.at[height], z_s.at[dz], z_r.at[height], at(z=height)).wait_recv()
    to_far.wait_recv()
    for g in range(2):
        total = zrecv[g * ZLO].astype(F32) + come[g].astype(F32)
        for k in range(1, ZLO):
            total += zrecv[g * ZLO + k].astype(F32)
        es[y, g] = total.astype(BF16)

    for d in (2, 1, 3):
        each = copy(es.at[y], es.at[y], es_s.at[d - 1], es_r.at[y], at(y=turn(y, d, NY)))
        each.start()
        sends.append(each)
    fetches[1].wait()
    for s in range(2):
        wanted[s] = jnp.full((8, COLS), st[s], jnp.int32)
    for d in (1, 3, 2):
        m = turn(y, d, NY)
        copy(es.at[m], es.at[m], es_s.at[d - 1], es_r.at[m], at(y=m)).wait_recv()

    def picked(m, s):
        total = jnp.zeros((ROWS, COLS), F32)
        for g in range(2):
            total += jnp.where(wanted[s][0:1] == 2 * (g * NX + x) + c, es[m, g].astype(F32), 0.0)
        return total.astype(BF16)

    for d, k in ((2, 0), (2, 1), (1, 0), (1, 1), (3, 0), (3, 1), (0, 1)):
        m, s = turn(x, d, NX), turn(c, k, 2)
        sel[d, k] = picked(m, s)
        each = copy(sel.at[d, k], srecv.at[x, c], sel_s.at[d, k], sel_r.at[x, c], at(x=m, c=s))
        each.start()
        sends.append(each)

    opposite = copy(es.at[:, 1 - zh], ep, ep_s, ep_r, at(z=turn(z, ZLO, NZ)))
    opposite.start()
    sends.append(opposite)

    srecv[x, c] = picked(x, c)
    for d, k in ((0, 1), (1, 0), (1, 1), (3, 0), (3, 1), (2, 0), (2, 1)):
        giver, core = turn(x, d, NX), turn(c, k, 2)
        copy(sel.at[d, k], srecv.at[giver, core], sel_s.at[d, k], sel_r.at[giver, core],
             at(x=giver, c=core) if d else sibling).wait_recv()
    total = jnp.zeros((ROWS, COLS), F32)
    for k in range(NX):
        for core in range(2):
            total += srecv[k, core].astype(F32)
    src[c, x, 0] = total.astype(BF16)

    groups = ((0, 1), (1, 2), (6, 2), (3, 1), (5, 1), (4, 1))

    def piece(s, m, group):
        return src.at[s, m, pl.ds(groups[group][0], groups[group][1])]

    for dz in (1, 7, 2, 6, 3, 5, 4):
        each = copy(src.at[c, x, 0], src.at[c, x, NZ - dz], up_s.at[dz], up_r.at[NZ - dz], at(z=turn(z, dz, NZ)))
        each.start()
        sends.append(each)

    def share(group, d):
        m = turn(x, NX - d, NX)
        each = copy(piece(c, m, group), piece(c, m, group), sib_s.at[d, group], sib_r.at[d, group], sibling)
        each.start()
        sends.append(each)

    def spread(group):
        for d in (2, 1, 3):
            each = copy(piece(c, x, group), piece(c, x, group), out_s.at[d - 1, group], out_r.at[d - 1, group],
                        at(x=turn(x, d, NX)))
            each.start()
            sends.append(each)
        share(group, 0)

    spread(0)

    def come_up(group):
        for k in range(groups[group][0], sum(groups[group])):
            copy(src.at[c, x, 0], src.at[c, x, k], up_s.at[1], up_r.at[k], at(z=turn(z, k, NZ))).wait_recv()
        spread(group)

    def come_out(group, d):
        m = turn(x, NX - d, NX)
        copy(piece(c, m, group), piece(c, m, group), out_s.at[d - 1, group], out_r.at[d - 1, group], at(x=m)).wait_recv()

    def come_shared(group, d):
        m = turn(x, NX - d, NX)
        copy(piece(1 - c, m, group), piece(1 - c, m, group), sib_s.at[d, group], sib_r.at[d, group], sibling).wait_recv()

    opposite.wait_recv()
    near = copy(ep, sink.at[c], sink_s, sink_r.at[c], sibling)
    far = copy(es.at[:, zh], sink.at[c], sink_s, sink_r.at[c], sibling)

    @pl.when(c == zh)
    def _():
        near.start()
        for m in range(NY):
            sink[c, m] = es[m, zh]

    @pl.when(c != zh)
    def _():
        far.start()
        sink[c] = ep[...]

    sends.append(near)
    come_up(1)
    come_up(2)

    copy(ep, sink.at[1 - c], sink_s, sink_r.at[1 - c], sibling).wait_recv()
    for t in range(2):
        left = sink[t].astype(F32).reshape(NY * ROWS, COLS).astype(BF16)
        for s in range(2):
            for k in range(4):
                value = jnp.dot(left, pcat[t, s, k], preferred_element_type=F32)
                value = value.reshape(NY, ROWS, COLS).astype(BF16)
                for m in range(NY):
                    half[s, m, 4 * t + k] = value[m]

    for group in (3, 4, 5):
        come_up(group)
    for group in (0, 1, 2):
        for d in (1, 3, 2):
            come_out(group, d)
            share(group, d)


    def flat(value):
        return value.astype(F32).reshape(NEV, COLS).astype(BF16)

    def finish(s, d):
        slot, m = d % 2, turn(x, NX - d, NX)
        heights = [(b % 2) * ZLO + b // 2 for b in range(NZ)]
        rows = [src[s, m, turn(height + NZ, -z, NZ)].astype(F32) for height in heights]
        rows = jnp.concatenate(rows, axis=0).astype(BF16)
        both[slot, :NEV] = rows
        both[slot, NEV:] = jnp.dot(rows, swap, preferred_element_type=F32).astype(BF16)
        value = lax.dot_general(flat(half[s, m]), both[slot], (((1,), (1,)), ((), ())), preferred_element_type=F32)
        value = value.reshape(2, 4, ROWS, COLS)
        for t in range(2):
            blocks[m, t, s] = value[t]

    finish(c, 0)
    for group in range(6):
        come_shared(group, 0)
    finish(1 - c, 0)
    for group in (3, 4, 5):
        for d in (1, 3, 2):
            come_out(group, d)
            share(group, d)
    for d in (1, 3, 2):
        finish(c, d)
    for d in (1, 3, 2):
        for group in range(6):
            come_shared(group, d)
        finish(1 - c, d)

    for each in sends:
        each.wait_send()


def exchanged(eigvecs, momenta, source_times, perambulator):
    dma = pltpu.SemaphoreType.DMA

    def vmem(*lead, kind=BF16):
        return pltpu.VMEM(lead + (ROWS, COLS), kind)

    return pl.pallas_call(
        exchange,
        out_shape=jax.ShapeDtypeStruct((NY, 2, 2, 4, ROWS, COLS), F32),
        in_specs=[pl.BlockSpec(memory_space=pltpu.HBM)] * 4,
        out_specs=pl.BlockSpec(memory_space=pltpu.VMEM),
        scratch_shapes=[
            vmem(2, 4, 8), vmem(2, 4, 8), pltpu.VMEM((2, COLS, COLS), BF16),
            pltpu.VMEM((2, SITES, COLS), BF16), pltpu.SMEM((NY, 3), jnp.int32), pltpu.SMEM((2,), jnp.int32),
            pltpu.VMEM((SITES, 8), F32), pltpu.VMEM((2, COLS, SITES), BF16), pltpu.VMEM((2, SITES, COLS), BF16),
            pltpu.VMEM((2, SITES, COLS), BF16),
            vmem(4, 8), vmem(4, 8), vmem(4, 8, kind=F32), vmem(3, 8), vmem(3, 8), vmem(8), vmem(8),
            pltpu.VMEM((2, 8, COLS), jnp.int32), vmem(4, 2), vmem(4, 2), vmem(4, 2), vmem(4), vmem(2, 4),
            pltpu.VMEM((2, 2, 4, COLS, COLS), BF16), vmem(8), vmem(2), vmem(2),
            dma((4,)), dma((2, 2)), dma((4,)), dma((4,)), dma((3, 2)), dma((3, 2)), dma((8,)), dma((8,)),
            dma((4, 2)), dma((4, 2)),
            dma((3,)), dma((4,)), dma, dma, dma, dma((2,)), dma((8,)), dma((8,)),
            dma((3, 6)), dma((3, 6)), dma((4, 6)), dma((4, 6)), dma((8,)), dma((8,)), dma, dma,
        ],
        compiler_params=pltpu.CompilerParams(
            collective_id=0, has_side_effects=True, vmem_limit_bytes=50 * 1024 * 1024
        ),
    )(eigvecs, momenta, source_times, perambulator)


def local(eigvecs, perambulator, momenta, source_times):
    def here(value):
        return pltpu.with_memory_space_constraint(value, pltpu.HBM)

    return exchanged(here(eigvecs), here(momenta), here(source_times), here(perambulator))


def solution(mesh):
    placed = (P("snk", ("src", "slab"), None), P("snk", "src", None, None, None), P(), P("src"))
    return jax.shard_map(
        local,
        mesh=mesh,
        in_specs=placed,
        out_specs=P(None, "snk", "src", None, "slab", None),
        check_vma=False,
    )
```
